32 devices in a mesh: groups: 2 (over x), lon: 16 (over z, y, core).
Axes of the slice: x: 2, y: 2, z: 4, core: 2. Of those that a mesh axis runs over, the one named last changes fastest.
Arguments:
- prior_state: bfloat16 [256, 226, 256], P(('groups', 'lon')), parts along dimension 0, may hold values from -6 to 6
- patch_embed: bfloat16 [2, 2, 226, 256], replicated, may hold values from -0.1875 to 0.1875
- conv_kernel: bfloat16 [2, 3, 3, 256], replicated, may hold values from -2 to 2
- conv_bias: bfloat16 [2, 256], replicated, may hold values from -2 to 2
- norm_gain: bfloat16 [2, 256], replicated, may hold values from 0.099609375 to 1.8984375
- mlp_up: bfloat16 [2, 256, 1024], replicated, may hold values from -0.375 to 0.375
- mlp_down: bfloat16 [2, 1024, 256], replicated, may hold values from -0.1875 to 0.1875
- patch_unembed: bfloat16 [256, 2, 2, 226], replicated, may hold values from -0.375 to 0.375
- emu_encode: bfloat16 [226, 1024], replicated, may hold values from -0.375 to 0.375
- chan_table: bfloat16 [22, 1024], replicated, may hold values from -5 to 5
- chan_head: bfloat16 [22, 1024], replicated, may hold values from -0.1875 to 0.1875
- head_bias: float32 [22], replicated, may hold values from -4 to 4
- obs_cells: int32 [131072], P(('groups', 'lon')), parts along dimension 0, may hold values from 0 to 2047
- obs_chans: int32 [131072], P(('groups', 'lon')), parts along dimension 0, may hold values from 0 to 21
- obs_values: float32 [131072], P(('groups', 'lon')), parts along dimension 0, may hold values from -6 to 6
- obs_counts: int32 [32], P(('groups', 'lon')), parts along dimension 0, may hold values from 1024 to 4096, as said below
Outputs:
- denoised: bfloat16 [256, 226, 256], P(('groups', 'lon')), parts along dimension 0
- state_gradient: float32 [256, 226, 256], P(('groups', 'lon')), parts along dimension 0
- innovations: float32 [131072], P(('groups', 'lon')), parts along dimension 0
The draws below stay inside these ranges and needn't reach their ends.
There are 2 independent parts, one for each index of `groups`. The reference program is written for one: setup_inputs(seed, part) draws one part's arguments, and reference() takes and returns one part's arrays. A program takes and returns all parts, laid end to end along the dimension named above; an argument that names none is the same for every part. Nothing has to cross between parts.
Inputs may be any that keep to these rules, and one draw needn't show every extreme that they name: `obs_counts`: slots of a device at or beyond its count are unused; some device is full and some holds exactly a quarter.
All inputs are finite; a program needn't handle non-finite values.
Results may differ from the reference program's by a relative error of at most 0.017.
Values may be sent and summed in bfloat16 or wider, within the bound.
No kernel may reach another device: no remote copies, remote signals or barrier semaphores. Data moves between devices by JAX's collectives and lax.ppermute only.
A program may use at most 128 MiB of HBM per device.

```python
import jax
import jax.numpy as jnp
from jax import lax

WIDTH = 256
HIDDEN_SIZE = 1024
EMU = 1024
NCHAN = 22
LAYERS = 2
LON_DEV = 8
LAT = 256
OBS_DEV = 4096
C = 226
CAP = 256
LON = 128
NOBS = 65536
N_LON = 16


def draw_obs_counts(key, part):
    first, second = jax.random.split(jax.random.fold_in(key, 11))
    counts = jax.random.randint(first, (N_LON,), OBS_DEV // 4, OBS_DEV + 1)
    order = jax.random.permutation(second, N_LON)
    positions = jnp.arange(N_LON, dtype=jnp.int32)
    counts = jnp.where(positions == order[0], OBS_DEV, counts)
    counts = jnp.where(positions == order[1], OBS_DEV // 4, counts)
    return counts.astype(jnp.int32)


def place_ends(values, rng, smallest, largest):
    shape = values.shape
    place = [jax.random.randint(jax.random.fold_in(rng, axis), (), 0, shape[axis]) for axis in range(len(shape))]
    values = values.at[tuple(place)].set(smallest)
    longest = shape.index(max(shape))
    place[longest] = (place[longest] + 1) % shape[longest]
    return values.at[tuple(place)].set(largest)


def block_levels(key, extent, cuts, least, top_value):
    def one(dim, blocks):
        heights = jax.random.uniform(jax.random.fold_in(jax.random.fold_in(key, 6), dim), (blocks,), jnp.float32, least / len(cuts), top_value / len(cuts))
        return jnp.repeat(jnp.exp(heights), extent[dim] // blocks).reshape((-1,) + (1,) * (len(extent) - dim - 1))

    level = one(*cuts[0])
    for cut in cuts[1:]:
        level = level * one(*cut)
    return level


def normal_values(stream_key, extent, width, limit, cuts=(), kind=jnp.bfloat16):
    factor_of = block_levels(stream_key, extent, cuts, -0.22, 0.18) if cuts else 1.0
    result = jax.random.normal(stream_key, extent, jnp.float32) * width * factor_of
    return jnp.minimum(jnp.maximum(result, -limit), limit).astype(kind)


def setup_inputs(seed: int = 0, part: int = 0) -> dict:
    seeds = jax.random.split(jax.random.key(seed), 17)
    part_keys = jax.random.split(jax.random.fold_in(seeds[16], part), 17)
    prior_state = normal_values(part_keys[0], (LON, C, LAT), 1.0, 6.0, ((0, 16),))
    patch_embed = normal_values(seeds[1], (2, 2, C, WIDTH), (4 * C) ** -0.5, 0.1875)
    conv_kernel = normal_values(seeds[2], (LAYERS, 3, 3, WIDTH), 0.35, 2.0)
    conv_bias = normal_values(seeds[3], (LAYERS, WIDTH), 0.3, 2.0)
    norm_gain = jnp.clip(1.0 + 0.18 * jax.random.normal(seeds[4], (LAYERS, WIDTH), jnp.float32), 0.099609375, 1.8984375).astype(jnp.bfloat16)
    mlp_up = normal_values(seeds[5], (LAYERS, WIDTH, HIDDEN_SIZE), WIDTH ** -0.5, 0.375)
    mlp_down = normal_values(seeds[6], (LAYERS, HIDDEN_SIZE, WIDTH), HIDDEN_SIZE ** -0.5, 0.1875)
    patch_unembed = normal_values(seeds[7], (WIDTH, 2, 2, C), WIDTH ** -0.5, 0.375)
    emu_encode = normal_values(seeds[8], (C, EMU), C ** -0.5, 0.375)
    chan_table = normal_values(seeds[9], (NCHAN, EMU), 1.0, 5.0)
    chan_head = normal_values(seeds[10], (NCHAN, EMU), EMU ** -0.5, 0.1875)
    head_bias = normal_values(seeds[11], (NCHAN,), 1.0, 4.0, (), jnp.float32)
    obs_cells = place_ends(jax.random.randint(part_keys[12], (NOBS,), 0, LON_DEV * LAT), jax.random.fold_in(part_keys[12], 1), 0, (LON_DEV * LAT) - 1).astype(jnp.int32)
    obs_chans = place_ends(jax.random.randint(part_keys[13], (NOBS,), 0, NCHAN), jax.random.fold_in(part_keys[13], 1), 0, NCHAN - 1).astype(jnp.int32)
    obs_values = normal_values(part_keys[14], (NOBS,), 1.0, 6.0, ((0, 16),), jnp.float32)
    obs_counts = draw_obs_counts(jax.random.fold_in(jax.random.fold_in(seeds[16], part), 71), part)
    return {"prior_state": prior_state, "patch_embed": patch_embed, "conv_kernel": conv_kernel, "conv_bias": conv_bias, "norm_gain": norm_gain, "mlp_up": mlp_up, "mlp_down": mlp_down, "patch_unembed": patch_unembed, "emu_encode": emu_encode, "chan_table": chan_table, "chan_head": chan_head, "head_bias": head_bias, "obs_cells": obs_cells, "obs_chans": obs_chans, "obs_values": obs_values, "obs_counts": obs_counts}


root_coef = 0.7978845608028654
cubic_coef = 0.044715
norm_eps = 1e-06

def widen(source):
    return lax.optimization_barrier(source).astype(jnp.float32)

def gelu_pair(pre_act):
    inner = root_coef * (pre_act + cubic_coef * pre_act * pre_act * pre_act)
    tangent = jnp.tanh(inner)
    value = 0.5 * pre_act * (1.0 + tangent)
    gelu_slope = 0.5 * (1.0 + tangent) + 0.5 * pre_act * (1.0 - tangent * tangent) * root_coef * (1.0 + 3.0 * cubic_coef * pre_act * pre_act)
    return (value, gelu_slope)

def lat_take(source, shift_by):
    if shift_by == 0:
        return source
    zero_col = jnp.zeros_like(source[..., :1])
    if shift_by < 0:
        return jnp.concatenate([zero_col, source[..., :-1]], axis=-1)
    return jnp.concatenate([source[..., 1:], zero_col], axis=-1)

def depthwise(padded, kernel, patch_rows):
    summed = jnp.zeros((patch_rows,) + padded.shape[1:], jnp.float32)
    for row_tap in range(3):
        rows_in = padded[row_tap:row_tap + patch_rows]
        for col_tap in range(3):
            summed = summed + kernel[row_tap, col_tap][None, :, None] * lat_take(rows_in, col_tap - 1)
    return summed

def embed_patches(prior_state, patch_embed):
    lon_rows, channels, lat_rows = prior_state.shape
    blocks = prior_state.astype(jnp.float32).reshape(lon_rows // 2, 2, channels, lat_rows // 2, 2)
    return jnp.einsum('iacjb,abce->iej', blocks, patch_embed.astype(jnp.float32))

def unembed_patches(hidden, patch_unembed):
    pieces = jnp.einsum('iej,eabc->iacjb', widen(hidden), patch_unembed.astype(jnp.float32))
    return pieces.reshape(pieces.shape[0] * 2, pieces.shape[2], pieces.shape[3] * 2)

def unembed_back(grad_round, patch_unembed):
    lon_rows, channels, lat_rows = grad_round.shape
    blocks = widen(grad_round).reshape(lon_rows // 2, 2, channels, lat_rows // 2, 2)
    return jnp.einsum('iacjb,eabc->iej', blocks, patch_unembed.astype(jnp.float32))

def embed_back(bottom_round, patch_embed):
    pieces = jnp.einsum('iej,abce->iacjb', widen(bottom_round), patch_embed.astype(jnp.float32))
    return pieces.reshape(pieces.shape[0] * 2, pieces.shape[2], pieces.shape[3] * 2)

def layer_forward(padded, kernel, conv_bias, norm_gain, mlp_up, mlp_down, patch_rows):
    conv_out = depthwise(widen(padded), kernel.astype(jnp.float32), patch_rows) + conv_bias.astype(jnp.float32)[None, :, None]
    inv_rms = lax.rsqrt(lax.optimization_barrier(jnp.mean(conv_out * conv_out, axis=1, keepdims=True)) + norm_eps)
    normed = (conv_out * inv_rms * norm_gain.astype(jnp.float32)[None, :, None]).astype(jnp.bfloat16)
    pre_act = jnp.einsum('iej,ef->ifj', widen(normed), mlp_up.astype(jnp.float32))
    activation, gelu_slope = gelu_pair(pre_act)
    activation = activation.astype(jnp.bfloat16)
    output = conv_out + jnp.einsum('ifj,fe->iej', widen(activation), mlp_down.astype(jnp.float32))
    return (output.astype(jnp.bfloat16), conv_out, inv_rms, gelu_slope)

def layer_backward(upstream, conv_out, inv_rms, gelu_slope, norm_gain, mlp_up, mlp_down):
    out_grad = upstream.astype(jnp.bfloat16)
    act_grad = jnp.einsum('iej,fe->ifj', widen(out_grad), mlp_down.astype(jnp.float32))
    pre_grad = (act_grad * gelu_slope).astype(jnp.bfloat16)
    norm_grad = jnp.einsum('ifj,ef->iej', widen(pre_grad), mlp_up.astype(jnp.float32))
    unit_norm = conv_out * inv_rms
    scaled_grad = norm_grad * norm_gain.astype(jnp.float32)[None, :, None]
    return upstream + inv_rms * (scaled_grad - unit_norm * lax.optimization_barrier(jnp.mean(scaled_grad * unit_norm, axis=1, keepdims=True)))

def radiance_obs(columns, obs_chans, obs_values, live_mask, emu_encode, chan_table, chan_head, head_bias):
    one_hot = (obs_chans[:, None] == jnp.arange(chan_table.shape[0], dtype=jnp.int32)[None, :]).astype(jnp.bfloat16)
    pre_act = jnp.dot(columns, emu_encode, preferred_element_type=jnp.float32) + jnp.dot(one_hot, chan_table, preferred_element_type=jnp.float32)
    head_rows = jnp.dot(one_hot, chan_head, preferred_element_type=jnp.float32)
    head_offset = lax.optimization_barrier(jnp.sum(one_hot.astype(jnp.float32) * head_bias[None, :], axis=1))
    activation, gelu_slope = gelu_pair(pre_act)
    predicted = lax.optimization_barrier(jnp.sum(activation * head_rows, axis=1)) + head_offset
    innovation = live_mask * (predicted - obs_values)
    pre_grad = (innovation[:, None] * head_rows * gelu_slope).astype(jnp.bfloat16)
    col_grad = jnp.dot(pre_grad, emu_encode.T, preferred_element_type=jnp.float32).astype(jnp.bfloat16)
    return (innovation, col_grad)

def radiance_blocks(columns, obs_chans, obs_values, live_mask, weights):
    slot_count = columns.shape[0]
    block_rows = min(slot_count, 1024)
    block_count = slot_count // block_rows

    def run_block(batch_items):
        return radiance_obs(batch_items[0], batch_items[1], batch_items[2], batch_items[3], weights[0], weights[1], weights[2], weights[3])
    innovation, col_grad = lax.map(run_block, (columns.reshape(block_count, block_rows, -1), obs_chans.reshape(block_count, block_rows), obs_values.reshape(block_count, block_rows), live_mask.reshape(block_count, block_rows)))
    return (innovation.reshape(slot_count), col_grad.reshape(slot_count, -1))

def reference(prior_state, patch_embed, conv_kernel, conv_bias, norm_gain, mlp_up, mlp_down, patch_unembed, emu_encode, chan_table, chan_head, head_bias, obs_cells, obs_chans, obs_values, obs_counts):
    hidden = embed_patches(prior_state, patch_embed).astype(jnp.bfloat16)
    patch_rows = hidden.shape[0]
    stored = []
    for depth in range(LAYERS):
        padded = jnp.concatenate([hidden[-1:], hidden, hidden[:1]], axis=0)
        hidden, conv_out, inv_rms, gelu_slope = layer_forward(padded, conv_kernel[depth], conv_bias[depth], norm_gain[depth], mlp_up[depth], mlp_down[depth], patch_rows)
        stored.append((conv_out, inv_rms, gelu_slope))
    denoised = (prior_state.astype(jnp.float32) + unembed_patches(hidden, patch_unembed)).astype(jnp.bfloat16)
    slots = jnp.arange(N_LON * OBS_DEV, dtype=jnp.int32)
    owners = slots // OBS_DEV
    within = slots % OBS_DEV
    flat_cells = (within // CAP * (LON_DEV * LAT) + obs_cells).astype(jnp.int32)
    live_mask = (within < obs_counts[owners]).astype(jnp.float32)
    col_table = jnp.transpose(denoised, (0, 2, 1)).reshape(LON * LAT, -1)
    columns = col_table[flat_cells]
    innovations, col_grad = radiance_blocks(columns, obs_chans, obs_values, live_mask, (emu_encode, chan_table, chan_head, head_bias))
    grad_cells = jnp.zeros((LON * LAT, columns.shape[1]), jnp.float32).at[flat_cells].add(col_grad.astype(jnp.float32))
    grad_hat = jnp.transpose(grad_cells.reshape(LON, LAT, -1), (0, 2, 1))
    upstream = unembed_back(grad_hat.astype(jnp.bfloat16), patch_unembed)
    for depth in reversed(range(LAYERS)):
        conv_out, inv_rms, gelu_slope = stored[depth]
        conv_grad = layer_backward(upstream, conv_out, inv_rms, gelu_slope, norm_gain[depth], mlp_up[depth], mlp_down[depth])
        padded = jnp.concatenate([conv_grad[-1:], conv_grad, conv_grad[:1]], axis=0)
        upstream = depthwise(padded, conv_kernel[depth].astype(jnp.float32)[::-1, ::-1], patch_rows)
    state_gradient = grad_hat + embed_back(upstream.astype(jnp.bfloat16), patch_embed)
    return (denoised, state_gradient, innovations)
```

```python
import functools

import jax
import jax.numpy as jnp
from jax import lax
from jax.experimental import pallas as pl
from jax.experimental.pallas import tpu as pltpu
from jax.sharding import PartitionSpec as P

LAYERS = 2
HALO = 2

root_coef = 0.7978845608028654
cubic_coef = 0.044715
norm_eps = 1e-06

F32 = jnp.float32
BF16 = jnp.bfloat16
GELU = jnp.bfloat16


def mm(a, b):
    return lax.dot_general(a, b, (((1,), (0,)), ((), ())), preferred_element_type=F32)


def mm_t(a, b):
    return lax.dot_general(a, b, (((1,), (1,)), ((), ())), preferred_element_type=F32)


def gelu_pair(pre):
    v = pre.astype(GELU)
    one = jnp.asarray(1.0, GELU)
    half = jnp.asarray(0.5, GELU)
    sq = v * v
    inner = v * (jnp.asarray(root_coef, GELU) + jnp.asarray(root_coef * cubic_coef, GELU) * sq)
    upper = half + half * jnp.tanh(inner)
    value = v * upper
    poly = jnp.asarray(2 * root_coef, GELU) + jnp.asarray(6 * root_coef * cubic_coef, GELU) * sq
    slope = upper + value * (one - upper) * poly
    return value, slope


def lat_split(size, dtype=BF16):
    row = lax.broadcasted_iota(jnp.int32, (size, size), 0)
    col = lax.broadcasted_iota(jnp.int32, (size, size), 1)
    half = size // 2
    want = jnp.where(row < half, 2 * row, 2 * (row - half) + 1)
    return jnp.where(col == want, 1.0, 0.0).astype(dtype)


def shift_rows(x, by):
    rows = x.shape[0]
    at = lax.broadcasted_iota(jnp.int32, x.shape, 0)
    if by == 1:
        return jnp.where(at == 0, 0.0, pltpu.roll(x, 1, 0))
    return jnp.where(at == rows - 1, 0.0, pltpu.roll(x, rows - 1, 0))


def conv_row(rows, taps):
    sums = []
    for q in range(3):
        total = taps[0][q] * rows[0]
        for p in (1, 2):
            total = total + taps[p][q] * rows[p]
        sums.append(total)
    return sums[1] + shift_rows(sums[0], 1) + shift_rows(sums[2], -1)


def load_taps(k_ref, layer, flip):
    def one(p, q):
        if flip:
            p, q = 2 - p, 2 - q
        return k_ref[p, q, :, :].astype(F32)[layer : layer + 1]

    return [[one(p, q) for q in range(3)] for p in range(3)]


def row_mean(x):
    width = x.shape[-1]
    return mm(x.astype(BF16), jnp.full((width, width), 1.0 / width, BF16))


def fill_lanes(xf, x_ref):
    chans, lon_rows, lat = x_ref.shape
    for k in range(lat // 128):
        part = x_ref[:, :, k * 128 : (k + 1) * 128].astype(F32)
        xf[k, 0 : chans * lon_rows, :] = part.reshape(chans * lon_rows, 128)
        xf[k, chans * lon_rows :, :] = jnp.zeros((xf.shape[1] - chans * lon_rows, 128), F32)


def lon_row(xf, lon, lon_rows):
    count = xf.shape[1] // lon_rows
    parts = [xf[k, pl.ds(lon, count, stride=lon_rows), :] for k in range(xf.shape[0])]
    return jnp.concatenate(parts, axis=1)


def put_lon_row(xf, lon, lon_rows, value):
    for k in range(xf.shape[0]):
        xf[k, pl.ds(lon, value.shape[0], stride=lon_rows), :] = value[:, k * 128 : (k + 1) * 128]


def embed_kernel(x_ref, w_ref, h_ref, first_ref, last_ref, xf, tcat):
    chans, lon_rows, lat = x_ref.shape
    padded = w_ref.shape[2]
    half = lat // 2
    fill_lanes(xf, x_ref)
    split = lat_split(lat)
    for lon in range(lon_rows):
        i, a = lon // 2, lon % 2
        tokens = mm_t(split, lon_row(xf, lon, lon_rows).astype(BF16)).astype(BF16)
        for b in range(2):
            tcat[i * half : (i + 1) * half, (2 * a + b) * padded : (2 * a + b + 1) * padded] = tokens[
                b * half : (b + 1) * half
            ]
    width = w_ref.shape[3]
    hidden = mm(tcat[...], w_ref[...].reshape(4 * padded, width)).astype(BF16)
    h_ref[...] = hidden
    first_ref[...] = hidden[: HALO * half]
    last_ref[...] = hidden[hidden.shape[0] - HALO * half :]


def split_kernel(x_ref, xp_ref, xf):
    chans, lon_rows, lat = x_ref.shape
    padded = xp_ref.shape[0]
    patch_rows = lon_rows // 2
    half = lat // 2
    fill_lanes(xf, x_ref)
    split = lat_split(lat)
    for lon in range(lon_rows):
        i, a = lon // 2, lon % 2
        part = mm_t(lon_row(xf, lon, lon_rows).astype(BF16), split).astype(BF16)
        for b in range(2):
            at = ((2 * a + b) * patch_rows + i) * half
            xp_ref[:, at : at + half] = part[:, b * half : (b + 1) * half]


def mlp_forward(layer, norm, conv, slope, up_ref, down_ref, store, tokens, block):
    for start in range(0, tokens, block):
        rows = pl.ds(start, block)
        value, tilt = gelu_pair(mm(norm[rows, :], up_ref[layer]))
        slope[rows, :] = tilt.astype(BF16)
        out = conv[rows, :] + mm(value.astype(BF16), down_ref[layer])
        store(start, out.astype(BF16))


def conv_norm_rows(count, source, layer, k_ref, bias_ref, gain_ref, conv, unit, scale, norm, half):
    taps = load_taps(k_ref, layer, False)
    bias = bias_ref[...].astype(F32)[layer : layer + 1]
    gain = gain_ref[...].astype(F32)[layer : layer + 1]

    def row(i, carry):
        out = conv_row([source[i + p].astype(F32) for p in range(3)], taps) + bias
        inv = lax.rsqrt(row_mean(out * out) + norm_eps)
        at = pl.ds(pl.multiple_of(i * half, half), half)
        u = out * inv
        conv[at, :] = out
        unit[at, :] = u
        scale[at, :] = inv
        norm[at, :] = (u * gain).astype(BF16)
        return carry

    lax.fori_loop(0, count, row, 0)


def mlp_backward(layer, upstream, unit, scale, slope, gain_ref, up_ref, down_ref):
    gain = gain_ref[...].astype(F32)[layer : layer + 1]
    pre = (mm_t(upstream.astype(BF16), down_ref[layer]) * slope.astype(F32)).astype(BF16)
    scaled = mm_t(pre, up_ref[layer]) * gain
    return upstream + scale * (scaled - unit * row_mean(scaled * unit))


def middle_kernel(
    h_ref, lo_ref, hi_ref, xp_ref, u_ref, k_ref, bias_ref, gain_ref, up_ref, down_ref,
    enc_ref, enct_ref, head_ref, headt_ref, hbias_ref, pay_ref,
    den_ref, innov_ref, cg_ref, first_ref, last_ref, unit0_ref, scale0_ref, slope0_ref, gradt_ref,
    h0, h1, conv, unit1, scale1, slope1, norm, h2, table, oht, gt, xf, gcell,
):
    chans, lon_rows, lat = den_ref.shape
    half = lat // 2
    patch_rows = lon_rows // 2
    padded = u_ref.shape[2]
    width = u_ref.shape[3]
    tokens = patch_rows * half
    wide = (patch_rows + 2) * half
    h0[0:HALO] = lo_ref[...].reshape(HALO, half, width)
    h0[HALO : HALO + patch_rows] = h_ref[...].reshape(patch_rows, half, width)
    h0[HALO + patch_rows :] = hi_ref[...].reshape(HALO, half, width)
    conv_norm_rows(
        patch_rows + 2, h0, 0, k_ref, bias_ref, gain_ref, conv, unit0_ref, scale0_ref, norm, half
    )

    def to_h1(start, out):
        h1[start // half : (start + out.shape[0]) // half] = out.reshape(-1, half, width)

    mlp_forward(0, norm, conv, slope0_ref, up_ref, down_ref, to_h1, wide, 2 * half)
    conv_norm_rows(
        patch_rows, h1, 1, k_ref, bias_ref, gain_ref, conv, unit1, scale1, norm, half
    )

    def to_h2(start, out):
        h2[start : start + out.shape[0], :] = out

    mlp_forward(1, norm, conv, slope1, up_ref, down_ref, to_h2, tokens, 2 * half)
    for ab in range(4):
        cols = slice(ab * tokens, (ab + 1) * tokens)
        table[:, cols] = (
            xp_ref[:, cols].astype(F32) + mm_t(u_ref[ab // 2, ab % 2], h2[...])
        ).astype(BF16)
    split = lat_split(lat)
    for lon in range(lon_rows):
        i, a = lon // 2, lon % 2
        at = [((2 * a + b) * patch_rows + i) * half for b in range(2)]
        both = jnp.concatenate([table[:, s : s + half] for s in at], axis=1)
        put_lon_row(xf, lon, lon_rows, mm(both, split))
    for k in range(lat // 128):
        part = xf[k, 0 : chans * lon_rows, :].reshape(chans, lon_rows, 128)
        den_ref[:, :, k * 128 : (k + 1) * 128] = part.astype(BF16)

    blocks, _, block = pay_ref.shape
    cells = lon_rows * lat
    head_pad = head_ref.shape[0]
    tail = padded - head_pad
    bias_col = hbias_ref[...]

    def radiance(p, carry):
        lanes = pl.ds(pl.multiple_of(p * block, block), block)
        pay = pay_ref[p]
        cell = pay[0:1].astype(jnp.int32)
        high = (cell // half).astype(F32)
        low = cell % half
        at = lax.broadcasted_iota(jnp.int32, (half, block), 0)
        key = jnp.where(at == low, high, -1.0).astype(BF16)
        for hi in range(cells // half):
            oht[hi * half : (hi + 1) * half, lanes] = jnp.where(
                key == jnp.asarray(hi, BF16), jnp.asarray(1, BF16), jnp.asarray(0, BF16)
            )
        columns = mm(table[...], oht[:, lanes])
        chan = pay[1:2].astype(jnp.int32)
        one_hot = jnp.where(
            lax.broadcasted_iota(jnp.int32, (head_pad, block), 0) == chan + (chans - tail), 1.0, 0.0
        )
        inputs = jnp.concatenate([columns[:tail], columns[tail:] + one_hot], axis=0).astype(BF16)
        pick = one_hot.astype(BF16)
        value, slope = gelu_pair(mm(enct_ref[...], inputs))
        heads = mm(headt_ref[...], pick).astype(GELU)
        found = mm(head_ref[...], value.astype(BF16)) + bias_col
        predicted = jnp.sum(found * one_hot, axis=0, keepdims=True)
        innov = pay[3:4] * (predicted - pay[2:3])
        innov_ref[pl.ds(p, 1), :] = innov
        grad = mm(enc_ref[...], (heads * slope).astype(BF16))
        gt[:, lanes] = (grad * innov).astype(BF16)
        return carry

    lax.fori_loop(0, blocks, radiance, 0)

    cell_block = 256

    def scatter(r, carry):
        rows = pl.ds(pl.multiple_of(r * cell_block, cell_block), cell_block)
        gcell[rows, :] = mm_t(oht[rows, :], gt[...]).astype(BF16)
        return carry

    lax.fori_loop(0, cells // cell_block, scatter, 0)
    eye = jnp.where(
        lax.broadcasted_iota(jnp.int32, (padded, padded), 0)
        == lax.broadcasted_iota(jnp.int32, (padded, padded), 1),
        1.0,
        0.0,
    ).astype(BF16)
    gradt_ref[...] = mm_t(eye, gcell[...]).astype(BF16)
    upstream = mm(gcell[0:tokens, :], u_ref[0, 0])
    for ab in range(1, 4):
        upstream = upstream + mm(gcell[ab * tokens : (ab + 1) * tokens, :], u_ref[ab // 2, ab % 2])
    grad = mlp_backward(
        1, upstream, unit1[...], scale1[...], slope1[...], gain_ref, up_ref, down_ref
    ).astype(BF16)
    cg_ref[...] = grad
    first_ref[...] = grad[: HALO * half]
    last_ref[...] = grad[tokens - HALO * half :]


def last_kernel(
    cg_ref, lo_ref, hi_ref, unit0_ref, scale0_ref, slope0_ref, gradt_ref,
    w_ref, k_ref, gain_ref, up_ref, down_ref, out_ref, c1, up1, c0, bottom, full, xf,
):
    rows_out, lat = out_ref.shape
    half = lat // 2
    padded = w_ref.shape[2]
    width = w_ref.shape[3]
    tokens = cg_ref.shape[0]
    patch_rows = tokens // half
    lon_rows = 2 * patch_rows
    chans = rows_out // lon_rows
    c1[0:HALO] = lo_ref[...].reshape(HALO, half, width)
    c1[HALO : HALO + patch_rows] = cg_ref[...].reshape(patch_rows, half, width)
    c1[HALO + patch_rows :] = hi_ref[...].reshape(HALO, half, width)
    taps = load_taps(k_ref, 1, True)

    def row1(i, carry):
        at = pl.ds(pl.multiple_of(i * half, half), half)
        up1[at, :] = conv_row([c1[i + p].astype(F32) for p in range(3)], taps)
        return carry

    lax.fori_loop(0, patch_rows + 2, row1, 0)
    for start in range(0, (patch_rows + 2) * half, 2 * half):
        at = pl.ds(start, 2 * half)
        grad = mlp_backward(
            0, up1[at, :], unit0_ref[at, :], scale0_ref[at, :], slope0_ref[at, :],
            gain_ref, up_ref, down_ref,
        )
        c0[start // half : start // half + 2] = grad.astype(BF16).reshape(2, half, width)
    taps0 = load_taps(k_ref, 0, True)

    def row0(i, carry):
        at = pl.ds(pl.multiple_of(i * half, half), half)
        bottom[at, :] = conv_row([c0[i + p].astype(F32) for p in range(3)], taps0).astype(BF16)
        return carry

    lax.fori_loop(0, patch_rows, row0, 0)
    for ab in range(4):
        cols = slice(ab * tokens, (ab + 1) * tokens)
        full[:, cols] = (
            gradt_ref[:, cols].astype(F32) + mm_t(w_ref[ab // 2, ab % 2], bottom[...])
        ).astype(BF16)
    split = lat_split(lat)
    for lon in range(lon_rows):
        i, a = lon // 2, lon % 2
        at = [((2 * a + b) * patch_rows + i) * half for b in range(2)]
        both = jnp.concatenate([full[:, s : s + half] for s in at], axis=1)
        put_lon_row(xf, lon, lon_rows, mm(both, split))
    for k in range(lat // 128):
        out_ref[:, k * 128 : (k + 1) * 128] = xf[k, 0:rows_out, :]


def call(kernel, outs, scratch, flops, nbytes, args, name):
    return pl.pallas_call(
        kernel,
        out_shape=[jax.ShapeDtypeStruct(shape, dtype) for shape, dtype in outs],
        scratch_shapes=[pltpu.VMEM(shape, dtype) for shape, dtype in scratch],
        cost_estimate=pl.CostEstimate(flops=flops, bytes_accessed=nbytes, transcendentals=0),
        name=name,
    )(*args)


def round_up(value, to):
    return -(-value // to) * to


def shards(
    prior_state, patch_embed, conv_kernel, conv_bias, norm_gain, mlp_up, mlp_down, patch_unembed,
    emu_encode, chan_table, chan_head, head_bias, obs_cells, obs_chans, obs_values, obs_counts,
):
    lon_size = lax.axis_size("lon")
    lon_rows, chans, lat = prior_state.shape
    slots = obs_cells.shape[0]
    per_peer = slots // lon_size
    width = patch_embed.shape[3]
    hidden_size = mlp_up.shape[2]
    emu, = emu_encode.shape[1:]
    nchan = chan_table.shape[0]
    half, patch_rows = lat // 2, lon_rows // 2
    tokens, cells = half * patch_rows, lat * lon_rows
    wide = tokens + 2 * half
    head_pad = 32
    padded = round_up(chans + nchan, 128)

    tile_lon, tile_lat = obs_cells // lat, obs_cells % lat
    place = ((tile_lon % 2 * 2 + tile_lat % 2) * patch_rows + tile_lon // 2) * half + tile_lat // 2
    live = (jnp.arange(slots, dtype=jnp.int32) < obs_counts[0]).astype(F32)
    sent = jnp.stack(
        [
            part.astype(F32).reshape(lon_size, per_peer)
            for part in (place, obs_chans, obs_values, live)
        ],
        axis=1,
    )
    pay = lax.all_to_all(sent, "lon", split_axis=0, concat_axis=0, tiled=True)
    group = max(1, 256 // per_peer)
    pay = pay.reshape(lon_size // group, group, 4, per_peer)
    pay = jnp.transpose(pay, (0, 2, 1, 3)).reshape(lon_size // group, 4, group * per_peer)

    forward = [(i, (i + 1) % lon_size) for i in range(lon_size)]
    backward = [(target, source) for source, target in forward]
    state = jnp.transpose(prior_state, (1, 0, 2))
    pad_c = ((0, 0), (0, 0), (0, padded - chans), (0, 0))
    w = jnp.pad(patch_embed, pad_c)
    u = jnp.pad(jnp.transpose(patch_unembed, (1, 2, 3, 0)), pad_c)
    taps = jnp.transpose(conv_kernel, (1, 2, 0, 3))
    hidden, first, last = call(
        embed_kernel,
        [((tokens, width), BF16), ((HALO * half, width), BF16), ((HALO * half, width), BF16)],
        [((lat // 128, padded * lon_rows, 128), F32), ((tokens, 4 * padded), BF16)],
        2 * tokens * 8 * padded * width, 2 * (state.size + w.size), (state, w), "embed",
    )
    low = lax.ppermute(last, "lon", forward)
    high = lax.ppermute(first, "lon", backward)
    (xp,) = call(
        split_kernel,
        [((padded, cells), BF16)],
        [((lat // 128, padded * lon_rows, 128), F32)],
        2 * tokens * 4 * padded * lat, 4 * state.size, (state,), "split",
    )
    rest = padded - chans - nchan
    enc = jnp.concatenate([emu_encode, chan_table, jnp.zeros((rest, emu), BF16)], axis=0)
    tail = padded - head_pad
    shift = chans - tail
    head = jnp.pad(chan_head, ((shift, head_pad - shift - nchan), (0, 0)))
    hbias = jnp.pad(head_bias, (shift, head_pad - shift - nchan)).reshape(head_pad, 1)
    (
        denoised, innov, grad, first, last, unit0, scale0, slope0, grad_t,
    ) = call(
        middle_kernel,
        [
            ((chans, lon_rows, lat), BF16),
            ((lon_size // group, group * per_peer), F32),
            ((tokens, width), BF16),
            ((HALO * half, width), BF16),
            ((HALO * half, width), BF16),
            ((wide, width), F32),
            ((wide, width), F32),
            ((wide, hidden_size), BF16),
            ((padded, cells), BF16),
        ],
        [
            ((patch_rows + 2 * HALO, half, width), BF16),
            ((patch_rows + 2, half, width), BF16),
            ((wide, width), F32),
            ((tokens, width), F32),
            ((tokens, width), F32),
            ((tokens, hidden_size), BF16),
            ((wide, width), BF16),
            ((tokens, width), BF16),
            ((padded, cells), BF16),
            ((cells, slots), BF16),
            ((padded, slots), BF16),
            ((lat // 128, padded * lon_rows, 128), F32),
            ((cells, padded), BF16),
        ],
        15 * 10**9, 10**7,
        (
            hidden, low, high, xp, u, taps, conv_bias, norm_gain, mlp_up, mlp_down,
            enc, enc.T, head, head.T, hbias, pay,
        ),
        "middle",
    )
    back = lax.ppermute(last, "lon", forward)
    ahead = lax.ppermute(first, "lon", backward)
    innovations = lax.all_to_all(
        innov.reshape(lon_size, per_peer), "lon", split_axis=0, concat_axis=0, tiled=True
    ).reshape(slots)
    (out,) = call(
        last_kernel,
        [((chans * lon_rows, lat), F32)],
        [
            ((patch_rows + 2 * HALO, half, width), BF16),
            ((wide, width), F32),
            ((patch_rows + 2, half, width), BF16),
            ((tokens, width), BF16),
            ((padded, cells), BF16),
            ((lat // 128, padded * lon_rows, 128), F32),
        ],
        4 * 10**9, 10**7,
        (grad, back, ahead, unit0, scale0, slope0, grad_t, w, taps, norm_gain, mlp_up, mlp_down),
        "last",
    )
    state_gradient = jnp.transpose(out.reshape(chans, lon_rows, lat), (1, 0, 2))
    return (jnp.transpose(denoised, (1, 0, 2)), state_gradient, innovations)


def solution(mesh):
    split = P(("groups", "lon"))
    placed = (split,) + (P(),) * 11 + (split,) * 4
    return jax.shard_map(
        shards, mesh=mesh, in_specs=placed, out_specs=(split,) * 3, check_vma=False
    )
```

```python
import functools

import jax
import jax.numpy as jnp
from jax import lax
from jax.experimental import pallas as pl
from jax.experimental.pallas import tpu as pltpu
from jax.sharding import PartitionSpec as P


HALO = 2

root_coef = 0.7978845608028654
cubic_coef = 0.044715
norm_eps = 1e-06

F32 = jnp.float32
BF16 = jnp.bfloat16
GELU = jnp.bfloat16


def mm(a, b):
    return lax.dot_general(a, b, (((1,), (0,)), ((), ())), preferred_element_type=F32)


def mm_t(a, b):
    return lax.dot_general(a, b, (((1,), (1,)), ((), ())), preferred_element_type=F32)


def gelu_pair(v):
    v = v.astype(GELU)
    one = jnp.asarray(1.0, GELU)
    sq = v * v
    cube = jnp.asarray(root_coef * cubic_coef, GELU) * sq
    inner = v * (jnp.asarray(root_coef, GELU) + cube)
    tangent = jnp.tanh(inner)
    upper = one + tangent
    poly = jnp.asarray(root_coef, GELU) + jnp.asarray(3 * root_coef * cubic_coef, GELU) * sq
    slope = upper * (one + v * poly * (one - tangent))
    return v * upper, slope


def copies(pairs, sems):
    started = [pltpu.make_async_copy(src, dst, sems.at[n]) for n, (src, dst) in enumerate(pairs)]
    for one in started:
        one.start()
    return started


def wide_dot(parts):
    return jnp.concatenate(parts, axis=1)


def lat_split(size, dtype=BF16):
    row = lax.broadcasted_iota(jnp.int32, (size, size), 0)
    col = lax.broadcasted_iota(jnp.int32, (size, size), 1)
    half = size // 2
    want = jnp.where(row < half, 2 * row, 2 * (row - half) + 1)
    return jnp.where(col == want, 1.0, 0.0).astype(dtype)


def shift_rows(x, by):
    rows = x.shape[0]
    at = lax.broadcasted_iota(jnp.int32, x.shape, 0)
    if by == 1:
        return jnp.where(at == 0, 0.0, pltpu.roll(x, 1, 0))
    return jnp.where(at == rows - 1, 0.0, pltpu.roll(x, rows - 1, 0))


def conv_row(rows, taps):
    sums = []
    for q in range(3):
        total = taps[0][q] * rows[0]
        for p in (1, 2):
            total = total + taps[p][q] * rows[p]
        sums.append(total)
    return sums[1] + shift_rows(sums[0], 1) + shift_rows(sums[2], -1)


def load_taps(k_ref, layer, flip):
    def one(p, q):
        if flip:
            p, q = 2 - p, 2 - q
        return k_ref[p, q, :, :].astype(F32)[layer : layer + 1]

    return [[one(p, q) for q in range(3)] for p in range(3)]


def whole(x, width):
    return jnp.concatenate([x] * (width // 128), axis=1)


def row_mean(x):
    width = x.shape[-1]
    return mm(x.astype(BF16), jnp.full((width, width), 1.0 / width, BF16))


def fill_lanes(xf, x, first, chans, lon_rows):
    for k in range(xf.shape[0]):
        part = x[first : first + chans, :, k * 128 : (k + 1) * 128].astype(F32)
        xf[k, first * lon_rows : (first + chans) * lon_rows, :] = part.reshape(chans * lon_rows, 128)


def lon_row(xf, lon, lon_rows):
    count = xf.shape[1] // lon_rows
    parts = [xf[k, pl.ds(lon, count, stride=lon_rows), :] for k in range(xf.shape[0])]
    return jnp.concatenate(parts, axis=1)


def put_lon_row(xf, lon, lon_rows, value):
    for k in range(xf.shape[0]):
        xf[k, pl.ds(lon, value.shape[0], stride=lon_rows), :] = value[:, k * 128 : (k + 1) * 128]


def fill_weights(out, w_ref, lanes):
    chans = w_ref.shape[1]
    for a in range(2):
        for k in range(out.shape[2] // 128):
            cols = slice(k * 128, (k + 1) * 128)
            lanes[k] = w_ref[a, :, :, cols].astype(F32).reshape(2 * chans, 128)
            for b in range(2):
                rows = lanes[k, pl.ds(b, chans, stride=2), :]
                out[2 * a + b, 0:chans, cols] = rows.astype(BF16)
    for ab in range(4):
        out[ab, chans:, :] = jnp.zeros((out.shape[1] - chans, out.shape[2]), BF16)


def embed_kernel(
    peers, *refs
):
    packed = peers is not None
    if packed:
        count_ref, cells_ref, chans_ref, values_ref, x_hbm, w_hbm = refs[:6]
        h_ref, first_ref, last_ref, pay_ref, xp_out, wp_out, *scratch = refs[6:]
    else:
        x_hbm, w_hbm, h_ref, first_ref, last_ref, xp_out, wp_out, *scratch = refs
    xf, tcat, wp, xp_ref, x_ref, w_ref, lanes, in_sems, sems = scratch
    chans, lon_rows, lat = x_ref.shape
    padded, width = wp.shape[1:]
    half = lat // 2
    edges = [chans * n // 4 for n in range(5)]
    spans = [pl.ds(lo, hi - lo) for lo, hi in zip(edges, edges[1:])]
    fetched = copies([(x_hbm.at[at], x_ref.at[at]) for at in spans] + [(w_hbm, w_ref)], in_sems)
    for k in range(lat // 128):
        xf[k, chans * lon_rows :, :] = jnp.zeros(((padded - chans) * lon_rows, 128), F32)
    for n in range(4):
        fetched[n].wait()
        fill_lanes(xf, x_ref, edges[n], edges[n + 1] - edges[n], lon_rows)
    split = lat_split(lat)
    for lon in range(lon_rows):
        i, a = lon // 2, lon % 2
        rows = lon_row(xf, lon, lon_rows).astype(BF16)
        tokens = mm_t(split, rows).astype(BF16)
        part = mm_t(rows, split).astype(BF16)
        for b in range(2):
            xp_ref[(2 * a + b) * (lon_rows // 2) + i] = part[:, b * half : (b + 1) * half]
            tcat[i * half : (i + 1) * half, (2 * a + b) * padded : (2 * a + b + 1) * padded] = tokens[
                b * half : (b + 1) * half
            ]
    fetched[4].wait()
    fill_weights(wp, w_ref, lanes)
    sent = copies([(xp_ref, xp_out), (wp, wp_out)], sems)
    hidden = mm(tcat[...], wp[...].reshape(4 * padded, width)).astype(BF16)
    h_ref[...] = hidden
    first_ref[...] = hidden[: HALO * half]
    last_ref[...] = hidden[hidden.shape[0] - HALO * half :]
    if not packed:
        for one in sent:
            one.wait()
        return
    rows, wide = cells_ref.shape
    per = rows // peers
    for part in range(per):
        at = pl.ds(part, peers, stride=per)
        cell = cells_ref[at, :]
        tile_lon, tile_lat = cell // lat, cell % lat
        place = (
            (tile_lon % 2 * 2 + tile_lat % 2) * (lon_rows // 2) + tile_lon // 2
        ) * half + tile_lat // 2
        slot = (
            lax.broadcasted_iota(jnp.int32, (peers, wide), 0) * (per * wide)
            + part * wide
            + lax.broadcasted_iota(jnp.int32, (peers, wide), 1)
        )
        live = jnp.where(slot < count_ref[0], 1.0, 0.0)
        kinds = (place.astype(F32), chans_ref[at, :].astype(F32), values_ref[at, :], live)
        for kind, value in enumerate(kinds):
            pay_ref[pl.ds(kind * per + part, peers, stride=4 * per), :] = value
    for one in sent:
        one.wait()


def mlp_forward(layer, norm, conv, slope, up_ref, down_ref, store, tokens, block):
    for start in range(0, tokens, block):
        rows = pl.ds(start, block)
        value, tilt = gelu_pair(mm(norm[rows, :], up_ref[layer]))
        slope[rows, :] = tilt.astype(BF16)
        out = conv[rows, :] + 0.5 * mm(value.astype(BF16), down_ref[layer])
        store(start, out.astype(BF16))


def conv_norm_rows(count, source, layer, k_ref, bias_ref, gain_ref, conv, unit, scale, norm, half):
    taps = load_taps(k_ref, layer, False)
    bias = bias_ref[...].astype(F32)[layer : layer + 1]
    gain = gain_ref[...].astype(F32)[layer : layer + 1]

    def row(i, carry):
        out = conv_row([source[i + p].astype(F32) for p in range(3)], taps) + bias
        inv = lax.rsqrt(row_mean(out * out) + norm_eps)
        at = pl.ds(pl.multiple_of(i * half, half), half)
        u = out * inv
        conv[at, :] = out
        unit[at, :] = u.astype(BF16)
        scale[at, :] = inv[:, 0:128]
        norm[at, :] = (u * gain).astype(BF16)
        return carry

    lax.fori_loop(0, count, row, 0)


def mlp_backward(upstream, unit, scale, slope, half_gain, up, down):
    pre = (mm_t(upstream.astype(BF16), down) * slope.astype(F32)).astype(BF16)
    scaled = mm_t(pre, up) * half_gain
    return upstream + scale * (scaled - unit * row_mean(scaled * unit))


def forward_kernel(
    h_ref, lo_ref, hi_ref, k_ref, bias_ref, gain_ref, xp_hbm, u_hbm, up_hbm, down_hbm,
    table_out, unit0_out, scale0_out, slope0_out, unit1_out, scale1_out, slope1_out, up_out,
    h0, h1, conv, norm, h2, up, xp_ref, u_ref, up_ref, down_ref,
    table_ref, unit0, scale0, slope0, unit1, scale1, slope1, lanes, sems, out_sems,
):
    fetched = copies(
        [(up_hbm, up_ref), (down_hbm, down_ref), (u_hbm, u_ref), (xp_hbm, xp_ref)], sems
    )
    _, _, half = table_ref.shape
    width = up.shape[2]
    tokens = h_ref.shape[0]
    patch_rows = tokens // half
    wide = (patch_rows + 2) * half
    h0[0:HALO] = lo_ref[...].reshape(HALO, half, width)
    h0[HALO : HALO + patch_rows] = h_ref[...].reshape(patch_rows, half, width)
    h0[HALO + patch_rows :] = hi_ref[...].reshape(HALO, half, width)
    conv_norm_rows(
        patch_rows + 2, h0, 0, k_ref, bias_ref, gain_ref, conv, unit0, scale0, norm, half
    )

    def to_h1(start, out):
        h1[start // half : (start + out.shape[0]) // half] = out.reshape(-1, half, width)

    fetched[0].wait()
    fetched[1].wait()
    mlp_forward(0, norm, conv, slope0, up_ref, down_ref, to_h1, wide, 2 * half)
    sent = copies(
        [(unit0, unit0_out), (scale0, scale0_out), (slope0, slope0_out)], out_sems.at[pl.ds(0, 3)]
    )
    fetched[2].wait()
    fill_weights(up, u_ref, lanes)
    sent += copies([(up, up_out)], out_sems.at[pl.ds(7, 1)])
    conv_norm_rows(
        patch_rows, h1, 1, k_ref, bias_ref, gain_ref, conv, unit1, scale1, norm, half
    )

    def to_h2(start, out):
        h2[start : start + out.shape[0], :] = out

    mlp_forward(1, norm, conv, slope1, up_ref, down_ref, to_h2, tokens, 2 * half)
    sent += copies(
        [(unit1, unit1_out), (scale1, scale1_out), (slope1, slope1_out)], out_sems.at[pl.ds(3, 3)]
    )
    fetched[3].wait()
    for ab in range(4):
        part = mm_t(up[ab], h2[...])
        for i in range(patch_rows):
            at = ab * patch_rows + i
            mine = part[:, i * half : (i + 1) * half]
            table_ref[at] = (xp_ref[at].astype(F32) + mine).astype(BF16)
    sent += copies([(table_ref, table_out)], out_sems.at[pl.ds(6, 1)])
    for one in sent:
        one.wait()


def is_cell(key, high):
    return jnp.where(key == jnp.asarray(high, BF16), jnp.asarray(1, BF16), jnp.asarray(0, BF16))


def identity(size):
    row = lax.broadcasted_iota(jnp.int32, (size, size), 0)
    col = lax.broadcasted_iota(jnp.int32, (size, size), 1)
    return jnp.where(row == col, 1.0, 0.0).astype(BF16)


def radiance_kernel(
    pay_ref, enc_ref, tab_ref, head_ref, hbias_ref, gain_ref,
    table_hbm, u_hbm, up_hbm, down_hbm, unit1_hbm, scale1_hbm, slope1_hbm,
    innov_ref, cg_ref, first_ref, last_ref, gradt_ref, den_out,
    enc, enct, heads, headst, keys, gt, gcell, up, xf, den, inputs, pre, out, value, slope,
    table_ref, up_ref, down_ref, unit1_ref, scale1_ref, slope1_ref, sems, out_sems,
):
    fetched = copies(
        [
            (table_hbm, table_ref),
            (u_hbm, up),
            (up_hbm.at[pl.ds(1, 1)], up_ref),
            (down_hbm.at[pl.ds(1, 1)], down_ref),
            (unit1_hbm, unit1_ref),
            (scale1_hbm, scale1_ref),
            (slope1_hbm, slope1_ref),
        ],
        sems,
    )
    chans, emu = enc_ref.shape
    nchan = tab_ref.shape[0]
    cell_blocks, padded, half = table_ref.shape
    blocks = pay_ref.shape[0]
    block = 2 * 128
    tokens, width = cg_ref.shape
    lon_rows, lat = den.shape[1:]
    patch_rows = lon_rows // 2
    one_at = round_up(chans, 8)
    tail = padded - heads.shape[1]
    shift = one_at - tail
    zeros = jnp.zeros((one_at - chans, 128), BF16)
    eye = identity(padded)
    for k in range(emu // 128):
        cols = slice(k * 128, (k + 1) * 128)
        enc[k, 0:chans, :] = enc_ref[:, cols]
        enc[k, chans:one_at, :] = zeros
        enc[k, one_at : one_at + nchan, :] = tab_ref[:, cols]
        enc[k, one_at + nchan :, :] = jnp.zeros((padded - one_at - nchan, 128), BF16)
        heads[k, 0:shift, :] = jnp.zeros((shift, 128), BF16)
        heads[k, shift : shift + nchan, :] = head_ref[:, cols]
        heads[k, shift + nchan :, :] = jnp.zeros((heads.shape[1] - shift - nchan, 128), BF16)
    for k in range(0, emu // 128, padded // 128):
        rows = slice(k * 128, k * 128 + padded)
        flip = mm_t(eye, wide_dot([enc[k + n] for n in range(padded // 128)])).astype(BF16)
        for n in range(padded // 128):
            enct[n, rows, :] = flip[:, n * 128 : (n + 1) * 128]
        headst[rows, :] = mm_t(eye, wide_dot([heads[k + n] for n in range(padded // 128)])).astype(BF16)
    rows = heads.shape[1]
    spot = lax.broadcasted_iota(jnp.int32, (rows, nchan), 0)
    lane = lax.broadcasted_iota(jnp.int32, (rows, nchan), 1)
    bias_row = jnp.broadcast_to(hbias_ref[...], (rows, nchan))
    bias_col = jnp.sum(jnp.where(spot == lane + shift, bias_row, 0.0), axis=1, keepdims=True)

    fetched[0].wait()
    split = lat_split(lat)
    for lon in range(lon_rows):
        i, a = lon // 2, lon % 2
        both = wide_dot([table_ref[(2 * a + b) * patch_rows + i] for b in range(2)])
        put_lon_row(xf, lon, lon_rows, mm(both, split))
    for k in range(lat // 128):
        part = xf[k, 0 : chans * lon_rows, :].reshape(chans, lon_rows, 128)
        den[:, :, k * 128 : (k + 1) * 128] = part.astype(BF16)
    sent = copies([(den, den_out)], out_sems)

    def row_of(pay, kind):
        return wide_dot([pay[2 * kind : 2 * kind + 1], pay[2 * kind + 1 : 2 * kind + 2]])

    def one_hot_of(pay):
        chan = row_of(pay, 1).astype(jnp.int32)
        at = lax.broadcasted_iota(jnp.int32, (rows, block), 0)
        return jnp.where(at == chan + shift, 1.0, 0.0)

    def gather(p):
        pay = pay_ref[p]
        cell = row_of(pay, 0).astype(jnp.int32)
        high = (cell // half).astype(F32)
        low = cell % half
        at = lax.broadcasted_iota(jnp.int32, (half, block), 0)
        key = jnp.where(at == low, high, -1.0).astype(BF16)
        for n in range(2):
            keys[2 * p + n] = key[:, n * 128 : (n + 1) * 128]
        picks = jnp.concatenate([is_cell(key, k) for k in range(cell_blocks)], axis=0)
        columns = mm(wide_dot([table_ref[k] for k in range(cell_blocks)]), picks)
        one_hot = one_hot_of(pay)
        inputs[0:tail, :] = columns[:tail].astype(BF16)
        inputs[tail:, :] = (columns[tail:] + one_hot).astype(BF16)

    def first_layer(p):
        one_hot = one_hot_of(pay_ref[p])
        pre[...] = mm(wide_dot([enct[n] for n in range(padded // 128)]), inputs[...]).astype(GELU)
        out[...] = mm(headst[:, 0:rows], one_hot.astype(BF16)).astype(GELU)

    def activate():
        for start in range(0, emu, 32):
            at = pl.ds(start, 32)
            act, tilt = gelu_pair(pre[at, :])
            value[at, :] = act.astype(BF16)
            slope[at, :] = (tilt * out[at, :]).astype(BF16)

    def finish(p):
        pay = pay_ref[p]
        found = mm(wide_dot([heads[k] for k in range(emu // 128)]), value[...])
        found = (0.5 * found + bias_col) * one_hot_of(pay)
        predicted = jnp.sum(found, axis=0, keepdims=True)
        innov = row_of(pay, 3) * (predicted - row_of(pay, 2))
        grad = mm(wide_dot([enc[k] for k in range(emu // 128)]), slope[...])
        grad = (grad * (0.5 * innov)).astype(BF16)
        for n in range(2):
            innov_ref[pl.ds(2 * p + n, 1), :] = innov[:, n * 128 : (n + 1) * 128]
            gt[2 * p + n] = grad[:, n * 128 : (n + 1) * 128]

    def steps(p, carry):
        finish(lax.rem(p + blocks - 3, blocks))
        activate()
        first_layer(jnp.clip(p - 1, 0, blocks - 1))
        gather(jnp.minimum(p, blocks - 1))
        return carry

    lax.fori_loop(0, blocks + 3, steps, 0)

    lane_blocks = keys.shape[0]

    def scatter(r, carry):
        key = wide_dot([keys[k] for k in range(lane_blocks)])
        high = (2 * r).astype(F32)
        picks = []
        for n in range(2):
            want = jnp.full((1, 1), high + n, F32).astype(BF16)
            picks.append(jnp.where(key == want, jnp.asarray(1, BF16), jnp.asarray(0, BF16)))
        lhs = jnp.concatenate(picks, axis=0)
        out = mm_t(lhs, wide_dot([gt[k] for k in range(lane_blocks)])).astype(BF16)
        at = pl.ds(pl.multiple_of(r * 2 * half, 2 * half), 2 * half)
        for n in range(padded // 128):
            gcell[n, at, :] = out[:, n * 128 : (n + 1) * 128]
        return carry

    lax.fori_loop(0, cell_blocks // 2, scatter, 0)
    for one in fetched[1:]:
        one.wait()
    flip = mm_t(eye, wide_dot([gcell[n] for n in range(padded // 128)])).astype(BF16)
    for k in range(cell_blocks):
        gradt_ref[k] = flip[:, k * half : (k + 1) * half]
    upstream = None
    for ab in range(4):
        at = slice(ab * tokens, (ab + 1) * tokens)
        part = mm(wide_dot([gcell[n, at, :] for n in range(padded // 128)]), up[ab])
        upstream = part if upstream is None else upstream + part
    grad = mlp_backward(
        upstream, unit1_ref[...].astype(F32), whole(scale1_ref[...], width), slope1_ref[...],
        0.5 * gain_ref[...].astype(F32)[1:2], up_ref[0], down_ref[0],
    ).astype(BF16)
    cg_ref[...] = grad
    first_ref[...] = grad[: HALO * half]
    last_ref[...] = grad[tokens - HALO * half :]
    sent[0].wait()


def last_kernel(
    cg_ref, lo_ref, hi_ref, k_ref, gain_ref,
    unit0_hbm, scale0_hbm, slope0_hbm, gradt_hbm, w_hbm, up_hbm, down_hbm, out_hbm,
    c1, up1, c0, bottom, full, xf, wp,
    unit0_ref, scale0_ref, slope0_ref, gradt_ref, up_ref, down_ref, sems, out_sems,
):
    wide, block = up1.shape[0], 2 * c1.shape[1]
    kept = [(slope0_hbm, slope0_ref), (unit0_hbm, unit0_ref), (scale0_hbm, scale0_ref)]
    pairs = [(down_hbm.at[pl.ds(0, 1)], down_ref), (up_hbm.at[pl.ds(0, 1)], up_ref)]
    for start in range(0, wide, block):
        pairs += [(src.at[pl.ds(start, block)], dst.at[pl.ds(start, block)]) for src, dst in kept]
    fetched = copies(pairs + [(w_hbm, wp), (gradt_hbm, gradt_ref)], sems)
    rows_out, lat = out_hbm.shape
    half = lat // 2
    _, width = wp.shape[1:]
    tokens = cg_ref.shape[0]
    patch_rows = tokens // half
    lon_rows = 2 * patch_rows
    c1[0:HALO] = lo_ref[...].reshape(HALO, half, width)
    c1[HALO : HALO + patch_rows] = cg_ref[...].reshape(patch_rows, half, width)
    c1[HALO + patch_rows :] = hi_ref[...].reshape(HALO, half, width)
    taps = load_taps(k_ref, 1, True)

    def row1(i, carry):
        at = pl.ds(pl.multiple_of(i * half, half), half)
        up1[at, :] = conv_row([c1[i + p].astype(F32) for p in range(3)], taps)
        return carry

    lax.fori_loop(0, patch_rows + 2, row1, 0)
    half_gain = 0.5 * gain_ref[...].astype(F32)[0:1]
    fetched[0].wait()
    fetched[1].wait()
    for start in range(0, wide, block):
        at = pl.ds(start, block)
        for n in range(3):
            fetched[2 + start // block * 3 + n].wait()
        grad = mlp_backward(
            up1[at, :], unit0_ref[at, :].astype(F32), whole(scale0_ref[at, :], width),
            slope0_ref[at, :],
            half_gain, up_ref[0], down_ref[0],
        )
        c0[start // half : start // half + 2] = grad.astype(BF16).reshape(2, half, width)
    taps0 = load_taps(k_ref, 0, True)

    def row0(i, carry):
        at = pl.ds(pl.multiple_of(i * half, half), half)
        bottom[at, :] = conv_row([c0[i + p].astype(F32) for p in range(3)], taps0).astype(BF16)
        return carry

    lax.fori_loop(0, patch_rows, row0, 0)
    fetched[-2].wait()
    fetched[-1].wait()
    for ab in range(4):
        part = mm_t(wp[ab], bottom[...])
        for i in range(patch_rows):
            at = ab * patch_rows + i
            mine = part[:, i * half : (i + 1) * half]
            full[at] = (gradt_ref[at].astype(F32) + mine).astype(BF16)
    split = lat_split(lat)
    for lon in range(lon_rows):
        i, a = lon // 2, lon % 2
        both = wide_dot([full[(2 * a + b) * patch_rows + i] for b in range(2)])
        put_lon_row(xf, lon, lon_rows, mm(both, split))
    sent = copies(
        [
            (xf.at[k, pl.ds(0, rows_out), :], out_hbm.at[:, pl.ds(k * 128, 128)])
            for k in range(lat // 128)
        ],
        out_sems,
    )
    for one in sent:
        one.wait()


ANY = pl.BlockSpec(memory_space=pl.ANY)
IN_VMEM = pl.BlockSpec(memory_space=pltpu.VMEM)
IN_SMEM = pl.BlockSpec(memory_space=pltpu.SMEM)


def call(kernel, outs, scratch, copies_in, copies_out, cost, smem=(), args=(), far=(), far_outs=(), limit=60):
    sems = [pltpu.SemaphoreType.DMA((n,)) for n in (copies_in, copies_out) if n]
    return pl.pallas_call(
        kernel,
        out_shape=[jax.ShapeDtypeStruct(shape, dtype) for shape, dtype in (*outs, *far_outs)],
        in_specs=[IN_SMEM] * len(smem) + [IN_VMEM] * len(args) + [ANY] * len(far),
        out_specs=[IN_VMEM] * len(outs) + [ANY] * len(far_outs),
        scratch_shapes=[pltpu.VMEM(shape, dtype) for shape, dtype in scratch] + sems,
        cost_estimate=pl.CostEstimate(
            flops=cost[0], bytes_accessed=cost[1], transcendentals=0
        ),
        compiler_params=pltpu.CompilerParams(vmem_limit_bytes=limit << 20),
    )(*smem, *args, *far)


def round_up(value, to):
    return -(-value // to) * to


BLOCK = 256


def shards(
    prior_state, patch_embed, conv_kernel, conv_bias, norm_gain, mlp_up, mlp_down, patch_unembed,
    emu_encode, chan_table, chan_head, head_bias, obs_cells, obs_chans, obs_values, obs_counts,
):
    lon_size = lax.axis_size("lon")
    lon_rows, chans, lat = prior_state.shape
    slots = obs_cells.shape[0]
    per_peer = slots // lon_size
    width = patch_embed.shape[3]
    hidden_size = mlp_up.shape[2]
    emu = emu_encode.shape[1]
    nchan = chan_table.shape[0]
    half, patch_rows = lat // 2, lon_rows // 2
    tokens, cells = half * patch_rows, lat * lon_rows
    wide = tokens + 2 * half
    head_pad = 32
    padded = round_up(chans + nchan, 256)
    packed = per_peer == BLOCK
    lanes = slots // 128
    state = jnp.transpose(prior_state, (1, 0, 2))
    u = jnp.transpose(patch_unembed, (1, 3, 2, 0))
    w = jnp.transpose(patch_embed, (0, 2, 1, 3))
    taps = jnp.transpose(conv_kernel, (1, 2, 0, 3))
    forward = [(i, (i + 1) % lon_size) for i in range(lon_size)]
    backward = [(target, source) for source, target in forward]

    halo = ((HALO * half, width), BF16)
    fat = ((wide, width), F32)
    fat_unit, thin_unit = ((wide, width), BF16), ((tokens, width), BF16)
    fat_scale, thin_scale = ((wide, 128), F32), ((tokens, 128), F32)
    fat_slope, thin_slope = ((wide, hidden_size), BF16), ((tokens, hidden_size), BF16)
    by_cell = ((cells // half, padded, half), BF16)
    rows_f32 = ((lat // 128, padded * lon_rows, 128), F32)
    maps = ((4, padded, width), BF16)
    lane_maps = ((width // 128, 2 * chans, 128), F32)
    maps_in = ((2, chans, 2, width), BF16)
    one_up, one_down = ((1, width, hidden_size), BF16), ((1, hidden_size, width), BF16)

    smem, args, outs = (), (), []
    if packed:
        smem = (obs_counts,)
        args = tuple(x.reshape(lanes, 128) for x in (obs_cells, obs_chans, obs_values))
        outs = [((lanes * 4, 128), F32)]
    hidden, first, last, *pay, xp, w = call(
        functools.partial(embed_kernel, lon_size if packed else None),
        [((tokens, width), BF16), halo, halo] + outs,
        [
            rows_f32, ((tokens, 4 * padded), BF16), maps, by_cell,
            ((chans, lon_rows, lat), BF16), maps_in, lane_maps,
        ],
        5, 2, (2 * tokens * 12 * padded * width, 4 * state.size),
        smem, args, (state, w), (by_cell, maps),
    )
    low = lax.ppermute(last, "lon", forward)
    high = lax.ppermute(first, "lon", backward)
    if packed:
        sent = pay[0].reshape(lon_size, 4 * per_peer // 128, 128)
    else:
        tile_lon, tile_lat = obs_cells // lat, obs_cells % lat
        place = (tile_lon % 2 * 2 + tile_lat % 2) * patch_rows + tile_lon // 2
        place = place * half + tile_lat // 2
        live = (jnp.arange(slots, dtype=jnp.int32) < obs_counts[0]).astype(F32)
        sent = jnp.stack(
            [
                part.astype(F32).reshape(lon_size, per_peer)
                for part in (place, obs_chans, obs_values, live)
            ],
            axis=1,
        )
    pay = lax.all_to_all(sent, "lon", split_axis=0, concat_axis=0, tiled=True)
    if not packed:
        group = BLOCK // per_peer
        pay = pay.reshape(lon_size // group, group, 4, per_peer)
        pay = jnp.transpose(pay, (0, 2, 1, 3)).reshape(lon_size // group, 8, 128)
    table, unit0, scale0, slope0, unit1, scale1, slope1, u = call(
        forward_kernel,
        [],
        [
            ((patch_rows + 2 * HALO, half, width), BF16),
            ((patch_rows + 2, half, width), BF16),
            fat,
            ((wide, width), BF16),
            ((tokens, width), BF16),
            maps, by_cell, maps_in,
            (mlp_up.shape, BF16), (mlp_down.shape, BF16),
            by_cell, fat_unit, fat_scale, fat_slope, thin_unit, thin_scale, thin_slope,
            lane_maps,
        ],
        4, 8, (3 * 10**9, 10**7),
        (), (hidden, low, high, taps, conv_bias, norm_gain), (xp, u, mlp_up, mlp_down),
        (by_cell, fat_unit, fat_scale, fat_slope, thin_unit, thin_scale, thin_slope, maps),
    )
    innov, grad, first, last, grad_t, denoised = call(
        radiance_kernel,
        [((lanes, 128), F32), ((tokens, width), BF16), halo, halo, by_cell],
        [
            ((emu // 128, padded, 128), BF16),
            ((padded // 128, emu, 128), BF16),
            ((emu // 128, head_pad, 128), BF16),
            ((emu, head_pad), BF16),
            ((lanes, half, 128), BF16),
            ((lanes, padded, 128), BF16),
            ((padded // 128, cells, 128), BF16),
            maps, rows_f32, ((chans, lon_rows, lat), BF16),
            ((padded, BLOCK), BF16), ((emu, BLOCK), GELU), ((emu, BLOCK), GELU),
            ((emu, BLOCK), BF16), ((emu, BLOCK), BF16),
            by_cell, one_up, one_down, thin_unit, thin_scale, thin_slope,
        ],
        7, 1, (14 * 10**9, 10**7),
        (),
        (pay, emu_encode, chan_table, chan_head, head_bias.reshape(1, nchan), norm_gain),
        (table, u, mlp_up, mlp_down, unit1, scale1, slope1),
        (((chans, lon_rows, lat), BF16),),
    )
    back = lax.ppermute(last, "lon", forward)
    ahead = lax.ppermute(first, "lon", backward)
    if packed:
        innov = innov.reshape(lon_size, per_peer // 128, 128)
    else:
        innov = innov.reshape(lon_size, per_peer)
    innovations = lax.all_to_all(innov, "lon", split_axis=0, concat_axis=0, tiled=True)
    (out,) = call(
        last_kernel,
        [],
        [
            ((patch_rows + 2 * HALO, half, width), BF16),
            fat,
            ((patch_rows + 2, half, width), BF16),
            ((tokens, width), BF16),
            by_cell, rows_f32, maps,
            fat_unit, fat_scale, fat_slope, by_cell, one_up, one_down,
        ],
        4 + 3 * (patch_rows + 2) // 2, lat // 128, (4 * 10**9, 10**7),
        (), (grad, back, ahead, taps, norm_gain),
        (unit0, scale0, slope0, grad_t, w, mlp_up, mlp_down),
        (((chans * lon_rows, lat), F32),),
    )
    state_gradient = jnp.transpose(out.reshape(chans, lon_rows, lat), (1, 0, 2))
    return (jnp.transpose(denoised, (1, 0, 2)), state_gradient, innovations.reshape(slots))


def solution(mesh):
    split = P(("groups", "lon"))
    placed = (split,) + (P(),) * 11 + (split,) * 4
    return jax.shard_map(
        shards, mesh=mesh, in_specs=placed, out_specs=(split,) * 3, check_vma=False
    )
```

```python
import functools

import jax
import jax.numpy as jnp
from jax import lax
from jax.experimental import pallas as pl
from jax.experimental.pallas import tpu as pltpu
from jax.sharding import PartitionSpec as P


HALO = 2

root_coef = 0.7978845608028654
cubic_coef = 0.044715
norm_eps = 1e-06

F32 = jnp.float32
BF16 = jnp.bfloat16
GELU = jnp.bfloat16


def mm(a, b):
    return lax.dot_general(a, b, (((1,), (0,)), ((), ())), preferred_element_type=F32)


def mm_t(a, b):
    return lax.dot_general(a, b, (((1,), (1,)), ((), ())), preferred_element_type=F32)


def gelu_pair(v):
    v = v.astype(GELU)
    one = jnp.asarray(1.0, GELU)
    sq = v * v
    cube = jnp.asarray(root_coef * cubic_coef, GELU) * sq
    inner = v * (jnp.asarray(root_coef, GELU) + cube)
    tangent = jnp.tanh(inner)
    upper = one + tangent
    poly = jnp.asarray(root_coef, GELU) + jnp.asarray(3 * root_coef * cubic_coef, GELU) * sq
    slope = upper * (one + v * poly * (one - tangent))
    return v * upper, slope


def copies(pairs, sems):
    started = [pltpu.make_async_copy(src, dst, sems.at[n]) for n, (src, dst) in enumerate(pairs)]
    for one in started:
        one.start()
    return started


def wide_dot(parts):
    return jnp.concatenate(parts, axis=1)


def lat_split(size, dtype=BF16):
    row = lax.broadcasted_iota(jnp.int32, (size, size), 0)
    col = lax.broadcasted_iota(jnp.int32, (size, size), 1)
    half = size // 2
    want = jnp.where(row < half, 2 * row, 2 * (row - half) + 1)
    return jnp.where(col == want, 1.0, 0.0).astype(dtype)


def shift_rows(x, by):
    rows = x.shape[0]
    at = lax.broadcasted_iota(jnp.int32, x.shape, 0)
    if by == 1:
        return jnp.where(at == 0, 0.0, pltpu.roll(x, 1, 0))
    return jnp.where(at == rows - 1, 0.0, pltpu.roll(x, rows - 1, 0))


def conv_row(rows, taps):
    sums = []
    for q in range(3):
        total = taps[0][q] * rows[0]
        for p in (1, 2):
            total = total + taps[p][q] * rows[p]
        sums.append(total)
    return sums[1] + shift_rows(sums[0], 1) + shift_rows(sums[2], -1)


def load_taps(k_ref, layer, flip):
    def one(p, q):
        if flip:
            p, q = 2 - p, 2 - q
        return k_ref[p, q, :, :].astype(F32)[layer : layer + 1]

    return [[one(p, q) for q in range(3)] for p in range(3)]


def whole(x, width):
    return jnp.concatenate([x] * (width // 128), axis=1)


def row_mean(x):
    width = x.shape[-1]
    return mm(x.astype(BF16), jnp.full((width, width), 1.0 / width, BF16))


def fill_lanes(xf, x, first, chans, lon_rows):
    for k in range(xf.shape[0]):
        part = x[first : first + chans, :, k * 128 : (k + 1) * 128].astype(F32)
        xf[k, first * lon_rows : (first + chans) * lon_rows, :] = part.reshape(chans * lon_rows, 128)


def lon_row(xf, lon, lon_rows):
    count = xf.shape[1] // lon_rows
    parts = [xf[k, pl.ds(lon, count, stride=lon_rows), :] for k in range(xf.shape[0])]
    return jnp.concatenate(parts, axis=1)


def put_lon_row(xf, lon, lon_rows, value, first=0):
    for k in range(xf.shape[0]):
        at = pl.ds(first * lon_rows + lon, value.shape[0], stride=lon_rows)
        xf[k, at, :] = value[:, k * 128 : (k + 1) * 128]


def fill_weights(out, w_ref, lanes):
    chans = w_ref.shape[1]
    for a in range(2):
        for k in range(out.shape[2] // 128):
            cols = slice(k * 128, (k + 1) * 128)
            lanes[k] = w_ref[a, :, :, cols].astype(F32).reshape(2 * chans, 128)
            for b in range(2):
                rows = lanes[k, pl.ds(b, chans, stride=2), :]
                out[2 * a + b, 0:chans, cols] = rows.astype(BF16)
    for ab in range(4):
        out[ab, chans:, :] = jnp.zeros((out.shape[1] - chans, out.shape[2]), BF16)


def embed_kernel(peers, fetch, ready, *refs):
    packed = peers is not None
    if packed:
        count_ref, cells_ref, chans_ref, values_ref, x_hbm, w_hbm = refs[:6]
        h_ref, first_ref, last_ref, pay_ref, xp_out, wp_out, *scratch = refs[6:]
    else:
        x_hbm, w_hbm, h_ref, first_ref, last_ref, xp_out, wp_out, *scratch = refs
    xf, tcat, wp, xp_ref, x_ref, w_ref, lanes, in_sems, sems = scratch
    chans, lon_rows, lat = x_ref.shape
    padded, width = wp.shape[1:]
    half = lat // 2
    edges = [chans * n // 4 for n in range(5)]
    spans = [pl.ds(lo, hi - lo) for lo, hi in zip(edges, edges[1:])]
    fetched = copies([(x_hbm.at[at], x_ref.at[at]) for at in spans] + [(w_hbm, w_ref)], in_sems)
    fetch()
    for k in range(lat // 128):
        xf[k, chans * lon_rows :, :] = jnp.zeros(((padded - chans) * lon_rows, 128), F32)
    for n in range(4):
        fetched[n].wait()
        fill_lanes(xf, x_ref, edges[n], edges[n + 1] - edges[n], lon_rows)
    split = lat_split(lat)
    sent = []
    for lon in range(lon_rows):
        i, a = lon // 2, lon % 2
        rows = lon_row(xf, lon, lon_rows).astype(BF16)
        tokens = mm_t(split, rows).astype(BF16)
        part = mm_t(rows, split).astype(BF16)
        for b in range(2):
            place = (2 * a + b) * (lon_rows // 2) + i
            xp_ref[place] = part[:, b * half : (b + 1) * half]
            here = pl.ds(place, 1)
            sent += copies([(xp_ref.at[here], xp_out.at[here])], sems.at[here])
            tcat[i * half : (i + 1) * half, (2 * a + b) * padded : (2 * a + b + 1) * padded] = tokens[
                b * half : (b + 1) * half
            ]
    fetched[4].wait()
    fill_weights(wp, w_ref, lanes)
    sent += copies([(wp, wp_out)], sems.at[pl.ds(2 * lon_rows, 1)])
    hidden = mm(tcat[...], wp[...].reshape(4 * padded, width)).astype(BF16)
    h_ref[...] = hidden
    first_ref[...] = hidden[: HALO * half]
    last_ref[...] = hidden[hidden.shape[0] - HALO * half :]
    ready()
    if not packed:
        return sent
    rows, wide = cells_ref.shape
    per = rows // peers
    for part in range(per):
        at = pl.ds(part, peers, stride=per)
        cell = cells_ref[at, :]
        tile_lon, tile_lat = cell // lat, cell % lat
        place = (
            (tile_lon % 2 * 2 + tile_lat % 2) * (lon_rows // 2) + tile_lon // 2
        ) * half + tile_lat // 2
        slot = (
            lax.broadcasted_iota(jnp.int32, (peers, wide), 0) * (per * wide)
            + part * wide
            + lax.broadcasted_iota(jnp.int32, (peers, wide), 1)
        )
        live = jnp.where(slot < count_ref[0], 1.0, 0.0)
        kinds = (place.astype(F32), chans_ref[at, :].astype(F32), values_ref[at, :], live)
        for kind, value in enumerate(kinds):
            pay_ref[pl.ds(kind * per + part, peers, stride=4 * per), :] = value
    return sent


def mlp_forward(layer, norm, conv, slope, up_ref, down_ref, store, tokens, block):
    for start in range(0, tokens, block):
        rows = pl.ds(start, block)
        value, tilt = gelu_pair(mm(norm[rows, :], up_ref[layer]))
        slope[rows, :] = tilt.astype(BF16)
        out = conv[rows, :] + 0.5 * mm(value.astype(BF16), down_ref[layer])
        store(start, out.astype(BF16))


def conv_norm_rows(count, source, layer, k_ref, bias_ref, gain_ref, conv, unit, scale, norm, half):
    taps = load_taps(k_ref, layer, False)
    bias = bias_ref[...].astype(F32)[layer : layer + 1]
    gain = gain_ref[...].astype(F32)[layer : layer + 1]

    def row(i, carry):
        out = conv_row([source[i + p].astype(F32) for p in range(3)], taps) + bias
        inv = lax.rsqrt(row_mean(out * out) + norm_eps)
        at = pl.ds(pl.multiple_of(i * half, half), half)
        u = out * inv
        conv[at, :] = out
        unit[at, :] = u.astype(BF16)
        scale[at, :] = inv[:, 0:128]
        norm[at, :] = (u * gain).astype(BF16)
        return carry

    lax.fori_loop(0, count, row, 0)


def mlp_backward(upstream, unit, scale, slope, half_gain, up, down):
    pre = (mm_t(upstream.astype(BF16), down) * slope.astype(F32)).astype(BF16)
    scaled = mm_t(pre, up) * half_gain
    return upstream + scale * (scaled - unit * row_mean(scaled * unit))


def forward_kernel(
    fetch, ready, h_ref, lo_ref, hi_ref, k_ref, bias_ref, gain_ref, xp_hbm, u_hbm, up_hbm, down_hbm,
    table_out, unit0_out, scale0_out, slope0_out, unit1_out, scale1_out, slope1_out, up_out,
    h0, h1, conv, norm, h2, up, xp_ref, u_ref, up_ref, down_ref,
    table_ref, unit0, scale0, slope0, unit1, scale1, slope1, lanes, sems, out_sems,
):
    fetch()
    low, high = pl.ds(0, 1), pl.ds(1, 1)
    early = copies(
        [(up_hbm.at[low], up_ref.at[low]), (down_hbm.at[low], down_ref.at[low])],
        sems.at[pl.ds(0, 2)],
    )
    _, _, half = table_ref.shape
    width = up.shape[2]
    tokens = h_ref.shape[0]
    patch_rows = tokens // half
    wide = (patch_rows + 2) * half
    ready()
    late = copies(
        [
            (u_hbm, u_ref),
            (up_hbm.at[high], up_ref.at[high]),
            (down_hbm.at[high], down_ref.at[high]),
            (xp_hbm, xp_ref),
        ],
        sems.at[pl.ds(2, 4)],
    )
    h0[0:HALO] = lo_ref[...].reshape(HALO, half, width)
    h0[HALO : HALO + patch_rows] = h_ref[...].reshape(patch_rows, half, width)
    h0[HALO + patch_rows :] = hi_ref[...].reshape(HALO, half, width)
    conv_norm_rows(
        patch_rows + 2, h0, 0, k_ref, bias_ref, gain_ref, conv, unit0, scale0, norm, half
    )

    def to_h1(start, out):
        h1[start // half : (start + out.shape[0]) // half] = out.reshape(-1, half, width)

    early[0].wait()
    early[1].wait()
    mlp_forward(0, norm, conv, slope0, up_ref, down_ref, to_h1, wide, 2 * half)
    sent = copies(
        [(unit0, unit0_out), (scale0, scale0_out), (slope0, slope0_out)], out_sems.at[pl.ds(0, 3)]
    )
    late[0].wait()
    fill_weights(up, u_ref, lanes)
    sent += copies([(up, up_out)], out_sems.at[pl.ds(7, 1)])
    conv_norm_rows(
        patch_rows, h1, 1, k_ref, bias_ref, gain_ref, conv, unit1, scale1, norm, half
    )

    def to_h2(start, out):
        h2[start : start + out.shape[0], :] = out

    late[1].wait()
    late[2].wait()
    mlp_forward(1, norm, conv, slope1, up_ref, down_ref, to_h2, tokens, 2 * half)
    sent += copies(
        [(unit1, unit1_out), (scale1, scale1_out), (slope1, slope1_out)], out_sems.at[pl.ds(3, 3)]
    )
    late[3].wait()
    for ab in range(4):
        part = mm_t(up[ab], h2[...])
        for i in range(patch_rows):
            at = ab * patch_rows + i
            mine = part[:, i * half : (i + 1) * half]
            table_ref[at] = (xp_ref[at].astype(F32) + mine).astype(BF16)
    return sent + copies([(table_ref, table_out)], out_sems.at[pl.ds(6, 1)])


def is_cell(key, high):
    return jnp.where(key == jnp.asarray(high, BF16), jnp.asarray(1, BF16), jnp.asarray(0, BF16))


def identity(size):
    row = lax.broadcasted_iota(jnp.int32, (size, size), 0)
    col = lax.broadcasted_iota(jnp.int32, (size, size), 1)
    return jnp.where(row == col, 1.0, 0.0).astype(BF16)


def radiance_kernel(
    fetch, ready, pay_ref, enc_ref, tab_ref, head_ref, hbias_ref, gain_ref,
    table_hbm, u_hbm, up_hbm, down_hbm, unit1_hbm, scale1_hbm, slope1_hbm,
    innov_ref, cg_ref, first_ref, last_ref, gradt_out, den_out,
    enc, enct, heads, headst, keys, gt, gcell, up, xf, den, inputs, pre, out, sums, slope,
    table_ref, up_ref, down_ref, unit1_ref, scale1_ref, slope1_ref, gradt_ref, sems, out_sems,
):
    fetch()
    fetched = copies(
        [
            (table_hbm, table_ref),
            (u_hbm, up),
            (up_hbm.at[pl.ds(1, 1)], up_ref),
            (down_hbm.at[pl.ds(1, 1)], down_ref),
            (unit1_hbm, unit1_ref),
            (scale1_hbm, scale1_ref),
            (slope1_hbm, slope1_ref),
        ],
        sems,
    )
    chans, emu = enc_ref.shape
    nchan = tab_ref.shape[0]
    cell_blocks, padded, half = table_ref.shape
    blocks = pay_ref.shape[0]
    block = 2 * 128
    tokens, width = cg_ref.shape
    lon_rows, lat = den.shape[1:]
    patch_rows = lon_rows // 2
    one_at = round_up(chans, 8)
    tail = padded - heads.shape[1]
    shift = one_at - tail
    ready()
    zeros = jnp.zeros((one_at - chans, 128), BF16)
    eye = identity(padded)
    for k in range(emu // 128):
        cols = slice(k * 128, (k + 1) * 128)
        enc[k, 0:chans, :] = enc_ref[:, cols]
        enc[k, chans:one_at, :] = zeros
        enc[k, one_at : one_at + nchan, :] = tab_ref[:, cols]
        enc[k, one_at + nchan :, :] = jnp.zeros((padded - one_at - nchan, 128), BF16)
        heads[k, 0:shift, :] = jnp.zeros((shift, 128), BF16)
        heads[k, shift : shift + nchan, :] = head_ref[:, cols]
        heads[k, shift + nchan :, :] = jnp.zeros((heads.shape[1] - shift - nchan, 128), BF16)
    headst[...] = jnp.zeros_like(headst)
    for k in range(0, emu // 128, padded // 128):
        rows = slice(k * 128, k * 128 + padded)
        flip = mm_t(eye, wide_dot([enc[k + n] for n in range(padded // 128)])).astype(BF16)
        for n in range(padded // 128):
            enct[n, rows, :] = flip[:, n * 128 : (n + 1) * 128]
        flip = mm_t(eye, wide_dot([heads[k + n] for n in range(padded // 128)])).astype(F32)
        headst[rows, 0:nchan] = flip[:, shift : shift + nchan]
    rows = heads.shape[1]
    spot = lax.broadcasted_iota(jnp.int32, (rows, nchan), 0)
    lane = lax.broadcasted_iota(jnp.int32, (rows, nchan), 1)
    bias_row = jnp.broadcast_to(hbias_ref[...], (rows, nchan))
    bias_col = jnp.sum(jnp.where(spot == lane + shift, bias_row, 0.0), axis=1, keepdims=True)

    fetched[0].wait()
    split = lat_split(lat)
    for lon in range(lon_rows):
        i, a = lon // 2, lon % 2
        both = wide_dot([table_ref[(2 * a + b) * patch_rows + i] for b in range(2)])
        put_lon_row(xf, lon, lon_rows, mm(both, split))
    for k in range(lat // 128):
        part = xf[k, 0 : chans * lon_rows, :].reshape(chans, lon_rows, 128)
        den[:, :, k * 128 : (k + 1) * 128] = part.astype(BF16)
    sent = copies([(den, den_out)], out_sems.at[pl.ds(0, 1)])

    def row_of(pay, kind):
        return wide_dot([pay[2 * kind : 2 * kind + 1], pay[2 * kind + 1 : 2 * kind + 2]])

    def one_hot_of(pay):
        chan = row_of(pay, 1).astype(jnp.int32)
        at = lax.broadcasted_iota(jnp.int32, (rows, block), 0)
        return jnp.where(at == chan + shift, 1.0, 0.0)

    def gather(p):
        pay = pay_ref[p]
        cell = row_of(pay, 0).astype(jnp.int32)
        high = (cell // half).astype(F32)
        low = cell % half
        at = lax.broadcasted_iota(jnp.int32, (half, block), 0)
        key = jnp.where(at == low, high, -1.0).astype(BF16)
        for n in range(2):
            keys[2 * p + n] = key[:, n * 128 : (n + 1) * 128]
        picks = jnp.concatenate([is_cell(key, k) for k in range(cell_blocks)], axis=0)
        columns = mm(wide_dot([table_ref[k] for k in range(cell_blocks)]), picks)
        one_hot = one_hot_of(pay)
        inputs[0:tail, :] = columns[:tail].astype(BF16)
        inputs[tail:, :] = (columns[tail:] + one_hot).astype(BF16)

    def first_layer(p):
        pre[...] = mm(wide_dot([enct[n] for n in range(padded // 128)]), inputs[...]).astype(GELU)
        for n in range(2):
            chan = pay_ref[p][2 + n : 3 + n].astype(jnp.int32)
            at = jnp.broadcast_to(chan, headst.shape)
            picked = jnp.take_along_axis(headst[...], at, axis=1, mode="promise_in_bounds")
            out[:, n * 128 : (n + 1) * 128] = picked

    def activate():
        chunk, group = 32, 4
        total = None
        for first in range(0, emu, chunk * group):
            terms = None
            for start in range(first, first + chunk * group, chunk):
                at = pl.ds(start, chunk)
                act, tilt = gelu_pair(pre[at, :])
                head = out[at, :].astype(GELU)
                slope[at, :] = (tilt * head).astype(BF16)
                terms = act * head if terms is None else terms + act * head
            terms = terms.astype(F32)
            total = terms if total is None else total + terms
        sums[...] = jnp.sum(total.reshape(chunk // 8, 8, block), axis=0)

    def finish(p):
        pay = pay_ref[p]
        bias = jnp.sum(bias_col * one_hot_of(pay), axis=0, keepdims=True)
        predicted = 0.5 * jnp.sum(sums[...], axis=0, keepdims=True) + bias
        innov = row_of(pay, 3) * (predicted - row_of(pay, 2))
        grad = mm(wide_dot([enc[k] for k in range(emu // 128)]), slope[...])
        grad = (grad * (0.5 * innov)).astype(BF16)
        for n in range(2):
            innov_ref[pl.ds(2 * p + n, 1), :] = innov[:, n * 128 : (n + 1) * 128]
            gt[2 * p + n] = grad[:, n * 128 : (n + 1) * 128]

    def step(p, least=0, most=4):
        if most > 3:
            finish(p - 3)
        if least < 3 <= most:
            activate()
        if least < 2 <= most:
            first_layer(p - 1)
        if least < 1:
            gather(p)

    for p in range(3):
        step(p, 0, p + 1)
    lax.fori_loop(3, blocks, lambda p, carry: (step(p), carry)[1], 0)
    for p in range(3):
        step(blocks + p, p + 1, 4)

    lane_blocks = keys.shape[0]

    count = 4

    def scatter(r, carry):
        key = wide_dot([keys[k] for k in range(lane_blocks)])
        high = (count * r).astype(F32)
        picks = []
        for n in range(count):
            want = jnp.full((1, 1), high + n, F32).astype(BF16)
            picks.append(jnp.where(key == want, jnp.asarray(1, BF16), jnp.asarray(0, BF16)))
        lhs = jnp.concatenate(picks, axis=0)
        total = mm_t(lhs, wide_dot([gt[k] for k in range(lane_blocks)])).astype(BF16)
        at = pl.ds(pl.multiple_of(r * count * half, count * half), count * half)
        for n in range(padded // 128):
            gcell[n, at, :] = total[:, n * 128 : (n + 1) * 128]
        return carry

    lax.fori_loop(0, cell_blocks // count, scatter, 0)
    for one in fetched[1:]:
        one.wait()
    flip = mm_t(eye, wide_dot([gcell[n] for n in range(padded // 128)])).astype(BF16)
    for k in range(cell_blocks):
        gradt_ref[k] = flip[:, k * half : (k + 1) * half]
    sent += copies([(gradt_ref, gradt_out)], out_sems.at[pl.ds(1, 1)])
    upstream = None
    for ab in range(4):
        at = slice(ab * tokens, (ab + 1) * tokens)
        part = mm(wide_dot([gcell[n, at, :] for n in range(padded // 128)]), up[ab])
        upstream = part if upstream is None else upstream + part
    grad = mlp_backward(
        upstream, unit1_ref[...].astype(F32), whole(scale1_ref[...], width), slope1_ref[...],
        0.5 * gain_ref[...].astype(F32)[1:2], up_ref[0], down_ref[0],
    ).astype(BF16)
    cg_ref[...] = grad
    first_ref[...] = grad[: HALO * half]
    last_ref[...] = grad[tokens - HALO * half :]
    return sent


def last_kernel(
    fetch, ready, cg_ref, lo_ref, hi_ref, k_ref, gain_ref,
    unit0_hbm, scale0_hbm, slope0_hbm, gradt_hbm, w_hbm, up_hbm, down_hbm, out_hbm,
    c1, up1, c0, bottom, full, xf, wp,
    unit0_ref, scale0_ref, slope0_ref, gradt_ref, up_ref, down_ref, sems, out_sems,
):
    fetch()
    wide, block = up1.shape[0], 2 * c1.shape[1]
    kept = [(slope0_hbm, slope0_ref), (unit0_hbm, unit0_ref), (scale0_hbm, scale0_ref)]
    early = copies(
        [(down_hbm.at[pl.ds(0, 1)], down_ref), (up_hbm.at[pl.ds(0, 1)], up_ref)], sems.at[pl.ds(0, 2)]
    )
    ready()
    pairs = []
    for start in range(0, wide, block):
        pairs += [(src.at[pl.ds(start, block)], dst.at[pl.ds(start, block)]) for src, dst in kept]
    late = copies(pairs + [(w_hbm, wp), (gradt_hbm, gradt_ref)], sems.at[pl.ds(2, len(pairs) + 2)])
    rows_out, lat = out_hbm.shape
    half = lat // 2
    padded, width = wp.shape[1:]
    tokens = cg_ref.shape[0]
    patch_rows = tokens // half
    lon_rows = 2 * patch_rows
    chans = rows_out // lon_rows
    c1[0:HALO] = lo_ref[...].reshape(HALO, half, width)
    c1[HALO : HALO + patch_rows] = cg_ref[...].reshape(patch_rows, half, width)
    c1[HALO + patch_rows :] = hi_ref[...].reshape(HALO, half, width)
    taps = load_taps(k_ref, 1, True)

    def row1(i, carry):
        at = pl.ds(pl.multiple_of(i * half, half), half)
        up1[at, :] = conv_row([c1[i + p].astype(F32) for p in range(3)], taps)
        return carry

    lax.fori_loop(0, patch_rows + 2, row1, 0)
    half_gain = 0.5 * gain_ref[...].astype(F32)[0:1]
    early[0].wait()
    early[1].wait()
    for start in range(0, wide, block):
        at = pl.ds(start, block)
        for n in range(3):
            late[start // block * 3 + n].wait()
        grad = mlp_backward(
            up1[at, :], unit0_ref[at, :].astype(F32), whole(scale0_ref[at, :], width),
            slope0_ref[at, :],
            half_gain, up_ref[0], down_ref[0],
        )
        c0[start // half : start // half + 2] = grad.astype(BF16).reshape(2, half, width)
    taps0 = load_taps(k_ref, 0, True)

    def row0(i, carry):
        at = pl.ds(pl.multiple_of(i * half, half), half)
        bottom[at, :] = conv_row([c0[i + p].astype(F32) for p in range(3)], taps0).astype(BF16)
        return carry

    lax.fori_loop(0, patch_rows, row0, 0)
    late[-2].wait()
    late[-1].wait()
    for ab in range(4):
        part = mm_t(wp[ab], bottom[...])
        for i in range(patch_rows):
            at = ab * patch_rows + i
            mine = part[:, i * half : (i + 1) * half]
            full[at] = (gradt_ref[at].astype(F32) + mine).astype(BF16)
    split = lat_split(lat)
    sent = []
    spans = [(0, padded // 2), (padded // 2, chans)]
    for n, (low, high) in enumerate(spans):
        for lon in range(lon_rows):
            i, a = lon // 2, lon % 2
            both = wide_dot([full[(2 * a + b) * patch_rows + i, low : low + padded // 2] for b in range(2)])
            put_lon_row(xf, lon, lon_rows, mm(both, split), low)
        at = pl.ds(low * lon_rows, (high - low) * lon_rows)
        sent += copies(
            [(xf.at[k, at, :], out_hbm.at[at, pl.ds(k * 128, 128)]) for k in range(lat // 128)],
            out_sems.at[pl.ds(n * (lat // 128), lat // 128)],
        )
    return sent


ANY = pl.BlockSpec(memory_space=pl.ANY)
IN_SMEM = pl.BlockSpec(memory_space=pltpu.SMEM)


def whole_copies(kernel, counts, *refs):
    parts, at = [], 0
    for count in counts:
        parts.append(refs[at : at + count])
        at += count
    smem, args, far, outs, far_outs, args_in, outs_in, scratch, arg_sems, out_sems = parts
    fetched = []

    def fetch():
        if args:
            fetched.extend(copies(list(zip(args, args_in)), arg_sems[0]))

    def ready():
        for one in fetched:
            one.wait()

    sent = kernel(fetch, ready, *smem, *args_in, *far, *outs_in, *far_outs, *scratch)
    if outs:
        sent = list(sent) + copies(list(zip(outs_in, outs)), out_sems[0])
    for one in sent:
        one.wait()


def call(kernel, outs, scratch, copies_in, copies_out, cost, smem=(), args=(), far=(), far_outs=()):
    sems = [pltpu.SemaphoreType.DMA((n,)) for n in (copies_in, copies_out) if n]
    own = [[pltpu.SemaphoreType.DMA((n,))] if n else [] for n in (len(args), len(outs))]
    counts = (
        len(smem), len(args), len(far), len(outs), len(far_outs), len(args), len(outs),
        len(scratch) + len(sems), len(own[0]), len(own[1]),
    )
    held = [(arg.shape, arg.dtype) for arg in args] + list(outs) + list(scratch)
    return pl.pallas_call(
        functools.partial(whole_copies, kernel, counts),
        out_shape=[jax.ShapeDtypeStruct(shape, dtype) for shape, dtype in (*outs, *far_outs)],
        in_specs=[IN_SMEM] * len(smem) + [ANY] * (len(args) + len(far)),
        out_specs=[ANY] * (len(outs) + len(far_outs)),
        scratch_shapes=[pltpu.VMEM(shape, dtype) for shape, dtype in held] + sems + own[0] + own[1],
        cost_estimate=pl.CostEstimate(
            flops=cost[0], bytes_accessed=cost[1], transcendentals=0
        ),
        compiler_params=pltpu.CompilerParams(vmem_limit_bytes=60 << 20),
    )(*smem, *args, *far)


def round_up(value, to):
    return -(-value // to) * to


BLOCK = 256


def shards(
    prior_state, patch_embed, conv_kernel, conv_bias, norm_gain, mlp_up, mlp_down, patch_unembed,
    emu_encode, chan_table, chan_head, head_bias, obs_cells, obs_chans, obs_values, obs_counts,
):
    lon_size = lax.axis_size("lon")
    lon_rows, chans, lat = prior_state.shape
    slots = obs_cells.shape[0]
    per_peer = slots // lon_size
    width = patch_embed.shape[3]
    hidden_size = mlp_up.shape[2]
    emu = emu_encode.shape[1]
    nchan = chan_table.shape[0]
    half, patch_rows = lat // 2, lon_rows // 2
    tokens, cells = half * patch_rows, lat * lon_rows
    wide = tokens + 2 * half
    head_pad = 32
    padded = round_up(chans + nchan, 256)
    packed = per_peer == BLOCK
    lanes = slots // 128
    state = jnp.transpose(prior_state, (1, 0, 2))
    u = jnp.transpose(patch_unembed, (1, 3, 2, 0))
    w = jnp.transpose(patch_embed, (0, 2, 1, 3))
    taps = jnp.transpose(conv_kernel, (1, 2, 0, 3))
    forward = [(i, (i + 1) % lon_size) for i in range(lon_size)]
    backward = [(target, source) for source, target in forward]

    halo = ((HALO * half, width), BF16)
    fat = ((wide, width), F32)
    fat_unit, thin_unit = ((wide, width), BF16), ((tokens, width), BF16)
    fat_scale, thin_scale = ((wide, 128), F32), ((tokens, 128), F32)
    fat_slope, thin_slope = ((wide, hidden_size), BF16), ((tokens, hidden_size), BF16)
    by_cell = ((cells // half, padded, half), BF16)
    rows_f32 = ((lat // 128, padded * lon_rows, 128), F32)
    maps = ((4, padded, width), BF16)
    lane_maps = ((width // 128, 2 * chans, 128), F32)
    maps_in = ((2, chans, 2, width), BF16)
    one_up, one_down = ((1, width, hidden_size), BF16), ((1, hidden_size, width), BF16)

    smem, args, outs = (), (), []
    if packed:
        smem = (obs_counts,)
        args = tuple(x.reshape(lanes, 128) for x in (obs_cells, obs_chans, obs_values))
        outs = [((lanes * 4, 128), F32)]
    hidden, first, last, *pay, xp, w = call(
        functools.partial(embed_kernel, lon_size if packed else None),
        [((tokens, width), BF16), halo, halo] + outs,
        [
            rows_f32, ((tokens, 4 * padded), BF16), maps, by_cell,
            ((chans, lon_rows, lat), BF16), maps_in, lane_maps,
        ],
        5, cells // half + 1, (2 * tokens * 12 * padded * width, 4 * state.size),
        smem, args, (state, w), (by_cell, maps),
    )
    low = lax.ppermute(last, "lon", forward)
    high = lax.ppermute(first, "lon", backward)
    if packed:
        sent = pay[0].reshape(lon_size, 4 * per_peer // 128, 128)
    else:
        tile_lon, tile_lat = obs_cells // lat, obs_cells % lat
        place = (tile_lon % 2 * 2 + tile_lat % 2) * patch_rows + tile_lon // 2
        place = place * half + tile_lat // 2
        live = (jnp.arange(slots, dtype=jnp.int32) < obs_counts[0]).astype(F32)
        sent = jnp.stack(
            [
                part.astype(F32).reshape(lon_size, per_peer)
                for part in (place, obs_chans, obs_values, live)
            ],
            axis=1,
        )
    pay = lax.all_to_all(sent, "lon", split_axis=0, concat_axis=0, tiled=True)
    if not packed:
        group = BLOCK // per_peer
        pay = pay.reshape(lon_size // group, group, 4, per_peer)
        pay = jnp.transpose(pay, (0, 2, 1, 3)).reshape(lon_size // group, 8, 128)
    table, unit0, scale0, slope0, unit1, scale1, slope1, u = call(
        forward_kernel,
        [],
        [
            ((patch_rows + 2 * HALO, half, width), BF16),
            ((patch_rows + 2, half, width), BF16),
            fat,
            ((wide, width), BF16),
            ((tokens, width), BF16),
            maps, by_cell, maps_in,
            (mlp_up.shape, BF16), (mlp_down.shape, BF16),
            by_cell, fat_unit, fat_scale, fat_slope, thin_unit, thin_scale, thin_slope,
            lane_maps,
        ],
        6, 8, (3 * 10**9, 10**7),
        (), (hidden, low, high, taps, conv_bias, norm_gain), (xp, u, mlp_up, mlp_down),
        (by_cell, fat_unit, fat_scale, fat_slope, thin_unit, thin_scale, thin_slope, maps),
    )
    innov, grad, first, last, grad_t, denoised = call(
        radiance_kernel,
        [((lanes, 128), F32), ((tokens, width), BF16), halo, halo],
        [
            ((emu // 128, padded, 128), BF16),
            ((padded // 128, emu, 128), BF16),
            ((emu // 128, head_pad, 128), BF16),
            ((emu, 128), F32),
            ((lanes, half, 128), BF16),
            ((lanes, padded, 128), BF16),
            ((padded // 128, cells, 128), BF16),
            maps, rows_f32, ((chans, lon_rows, lat), BF16),
            ((padded, BLOCK), BF16), ((emu, BLOCK), GELU), ((emu, BLOCK), F32),
            ((8, BLOCK), F32), ((emu, BLOCK), BF16),
            by_cell, one_up, one_down, thin_unit, thin_scale, thin_slope, by_cell,
        ],
        7, 2, (14 * 10**9, 10**7),
        (),
        (pay, emu_encode, chan_table, chan_head, head_bias.reshape(1, nchan), norm_gain),
        (table, u, mlp_up, mlp_down, unit1, scale1, slope1),
        (by_cell, ((chans, lon_rows, lat), BF16)),
    )
    back = lax.ppermute(last, "lon", forward)
    ahead = lax.ppermute(first, "lon", backward)
    if packed:
        innov = innov.reshape(lon_size, per_peer // 128, 128)
    else:
        innov = innov.reshape(lon_size, per_peer)
    innovations = lax.all_to_all(innov, "lon", split_axis=0, concat_axis=0, tiled=True)
    (out,) = call(
        last_kernel,
        [],
        [
            ((patch_rows + 2 * HALO, half, width), BF16),
            fat,
            ((patch_rows + 2, half, width), BF16),
            ((tokens, width), BF16),
            by_cell, rows_f32, maps,
            fat_unit, fat_scale, fat_slope, by_cell, one_up, one_down,
        ],
        4 + 3 * (patch_rows + 2) // 2, 2 * (lat // 128), (4 * 10**9, 10**7),
        (), (grad, back, ahead, taps, norm_gain),
        (unit0, scale0, slope0, grad_t, w, mlp_up, mlp_down),
        (((chans * lon_rows, lat), F32),),
    )
    state_gradient = jnp.transpose(out.reshape(chans, lon_rows, lat), (1, 0, 2))
    return (jnp.transpose(denoised, (1, 0, 2)), state_gradient, innovations.reshape(slots))


def solution(mesh):
    split = P(("groups", "lon"))
    placed = (split,) + (P(),) * 11 + (split,) * 4
    return jax.shard_map(
        shards, mesh=mesh, in_specs=placed, out_specs=(split,) * 3, check_vma=False
    )
```

```python
import functools

import jax
import jax.numpy as jnp
from jax import lax
from jax.experimental import pallas as pl
from jax.experimental.pallas import tpu as pltpu
from jax.sharding import PartitionSpec as P


HALO = 2

root_coef = 0.7978845608028654
cubic_coef = 0.044715
norm_eps = 1e-06

F32 = jnp.float32
BF16 = jnp.bfloat16
GELU = jnp.bfloat16


def mm(a, b):
    return lax.dot_general(a, b, (((1,), (0,)), ((), ())), preferred_element_type=F32)


def mm_t(a, b):
    return lax.dot_general(a, b, (((1,), (1,)), ((), ())), preferred_element_type=F32)


def gelu_pair(v):
    v = v.astype(GELU)
    one = jnp.asarray(1.0, GELU)
    sq = v * v
    cube = jnp.asarray(root_coef * cubic_coef, GELU) * sq
    inner = v * (jnp.asarray(root_coef, GELU) + cube)
    tangent = jnp.tanh(inner)
    upper = one + tangent
    poly = jnp.asarray(root_coef, GELU) + jnp.asarray(3 * root_coef * cubic_coef, GELU) * sq
    slope = upper * (one + v * poly * (one - tangent))
    return v * upper, slope


def copies(pairs, sems):
    started = [pltpu.make_async_copy(src, dst, sems.at[n]) for n, (src, dst) in enumerate(pairs)]
    for one in started:
        one.start()
    return started


def wide_dot(parts):
    return jnp.concatenate(parts, axis=1)


def lat_split(size, dtype=BF16):
    row = lax.broadcasted_iota(jnp.int32, (size, size), 0)
    col = lax.broadcasted_iota(jnp.int32, (size, size), 1)
    half = size // 2
    want = jnp.where(row < half, 2 * row, 2 * (row - half) + 1)
    return jnp.where(col == want, 1.0, 0.0).astype(dtype)


def shift_rows(x, by):
    rows = x.shape[0]
    at = lax.broadcasted_iota(jnp.int32, x.shape, 0)
    if by == 1:
        return jnp.where(at == 0, 0.0, pltpu.roll(x, 1, 0))
    return jnp.where(at == rows - 1, 0.0, pltpu.roll(x, rows - 1, 0))


def conv_row(rows, taps):
    sums = []
    for q in range(3):
        total = taps[0][q] * rows[0]
        for p in (1, 2):
            total = total + taps[p][q] * rows[p]
        sums.append(total)
    return sums[1] + shift_rows(sums[0], 1) + shift_rows(sums[2], -1)


def load_taps(k_ref, layer, flip):
    def one(p, q):
        if flip:
            p, q = 2 - p, 2 - q
        return k_ref[p, q, :, :].astype(F32)[layer : layer + 1]

    return [[one(p, q) for q in range(3)] for p in range(3)]


def whole(x, width):
    return jnp.concatenate([x] * (width // 128), axis=1)


def row_mean(x):
    width = x.shape[-1]
    return mm(x.astype(BF16), jnp.full((width, width), 1.0 / width, BF16))


def fill_lanes(xf, x, first, chans, lon_rows):
    for k in range(xf.shape[0]):
        part = x[first : first + chans, :, k * 128 : (k + 1) * 128].astype(F32)
        xf[k, first * lon_rows : (first + chans) * lon_rows, :] = part.reshape(chans * lon_rows, 128)


def lon_row(xf, lon, lon_rows):
    count = xf.shape[1] // lon_rows
    parts = [xf[k, pl.ds(lon, count, stride=lon_rows), :] for k in range(xf.shape[0])]
    return jnp.concatenate(parts, axis=1)


def put_lon_row(xf, lon, lon_rows, value, first=0):
    for k in range(xf.shape[0]):
        at = pl.ds(first * lon_rows + lon, value.shape[0], stride=lon_rows)
        xf[k, at, :] = value[:, k * 128 : (k + 1) * 128]


def fill_weights(out, w_ref, lanes):
    chans = w_ref.shape[1]
    for a in range(2):
        for k in range(out.shape[2] // 128):
            cols = slice(k * 128, (k + 1) * 128)
            lanes[k] = w_ref[a, :, :, cols].astype(F32).reshape(2 * chans, 128)
            for b in range(2):
                rows = lanes[k, pl.ds(b, chans, stride=2), :]
                out[2 * a + b, 0:chans, cols] = rows.astype(BF16)
    for ab in range(4):
        out[ab, chans:, :] = jnp.zeros((out.shape[1] - chans, out.shape[2]), BF16)


def embed_kernel(peers, fetch, ready, *refs):
    packed = peers is not None
    if packed:
        count_ref, cells_ref, chans_ref, values_ref, x_hbm, w_hbm = refs[:6]
        h_ref, first_ref, last_ref, pay_ref, xp_out, wp_out, *scratch = refs[6:]
    else:
        x_hbm, w_hbm, h_ref, first_ref, last_ref, xp_out, wp_out, *scratch = refs
    xf, tcat, wp, xp_ref, x_ref, w_ref, lanes, in_sems, sems = scratch
    chans, lon_rows, lat = x_ref.shape
    padded, width = wp.shape[1:]
    half = lat // 2
    edges = [chans * n // 4 for n in range(5)]
    spans = [pl.ds(lo, hi - lo) for lo, hi in zip(edges, edges[1:])]
    fetched = copies([(x_hbm.at[at], x_ref.at[at]) for at in spans] + [(w_hbm, w_ref)], in_sems)
    fetch()
    for k in range(lat // 128):
        xf[k, chans * lon_rows :, :] = jnp.zeros(((padded - chans) * lon_rows, 128), F32)
    for n in range(4):
        fetched[n].wait()
        fill_lanes(xf, x_ref, edges[n], edges[n + 1] - edges[n], lon_rows)
    split = lat_split(lat)
    sent = []
    for lon in range(lon_rows):
        i, a = lon // 2, lon % 2
        rows = lon_row(xf, lon, lon_rows).astype(BF16)
        tokens = mm_t(split, rows).astype(BF16)
        part = mm_t(rows, split).astype(BF16)
        for b in range(2):
            place = (2 * a + b) * (lon_rows // 2) + i
            xp_ref[place] = part[:, b * half : (b + 1) * half]
            here = pl.ds(place, 1)
            sent += copies([(xp_ref.at[here], xp_out.at[here])], sems.at[here])
            tcat[i * half : (i + 1) * half, (2 * a + b) * padded : (2 * a + b + 1) * padded] = tokens[
                b * half : (b + 1) * half
            ]
    fetched[4].wait()
    fill_weights(wp, w_ref, lanes)
    sent += copies([(wp, wp_out)], sems.at[pl.ds(2 * lon_rows, 1)])
    hidden = mm(tcat[...], wp[...].reshape(4 * padded, width)).astype(BF16)
    h_ref[...] = hidden
    first_ref[...] = hidden[: HALO * half]
    last_ref[...] = hidden[hidden.shape[0] - HALO * half :]
    ready()
    if not packed:
        return sent
    rows, wide = cells_ref.shape
    per = rows // peers
    for part in range(per):
        at = pl.ds(part, peers, stride=per)
        cell = cells_ref[at, :]
        tile_lon, tile_lat = cell // lat, cell % lat
        place = (
            (tile_lon % 2 * 2 + tile_lat % 2) * (lon_rows // 2) + tile_lon // 2
        ) * half + tile_lat // 2
        slot = (
            lax.broadcasted_iota(jnp.int32, (peers, wide), 0) * (per * wide)
            + part * wide
            + lax.broadcasted_iota(jnp.int32, (peers, wide), 1)
        )
        live = jnp.where(slot < count_ref[0], 1.0, 0.0)
        kinds = (place.astype(F32), chans_ref[at, :].astype(F32), values_ref[at, :], live)
        for kind, value in enumerate(kinds):
            pay_ref[pl.ds(kind * per + part, peers, stride=4 * per), :] = value
    return sent


def mlp_forward(layer, norm, conv, slope, up_ref, down_ref, store, tokens, block):
    for start in range(0, tokens, block):
        rows = pl.ds(start, block)
        value, tilt = gelu_pair(mm(norm[rows, :], up_ref[layer]))
        slope[rows, :] = tilt.astype(BF16)
        out = conv[rows, :] + 0.5 * mm(value.astype(BF16), down_ref[layer])
        store(start, out.astype(BF16))


def conv_norm_rows(count, source, layer, k_ref, bias_ref, gain_ref, conv, unit, scale, norm, half):
    taps = load_taps(k_ref, layer, False)
    bias = bias_ref[...].astype(F32)[layer : layer + 1]
    gain = gain_ref[...].astype(F32)[layer : layer + 1]

    def row(i, carry):
        out = conv_row([source[i + p].astype(F32) for p in range(3)], taps) + bias
        inv = lax.rsqrt(row_mean(out * out) + norm_eps)
        at = pl.ds(pl.multiple_of(i * half, half), half)
        u = out * inv
        conv[at, :] = out
        unit[at, :] = u.astype(BF16)
        scale[at, :] = inv[:, 0:128]
        norm[at, :] = (u * gain).astype(BF16)
        return carry

    lax.fori_loop(0, count, row, 0)


def mlp_backward(upstream, unit, scale, slope, half_gain, up, down):
    pre = (mm_t(upstream.astype(BF16), down) * slope.astype(F32)).astype(BF16)
    scaled = mm_t(pre, up) * half_gain
    return upstream + scale * (scaled - unit * row_mean(scaled * unit))


def forward_kernel(
    fetch, ready, h_ref, lo_ref, hi_ref, k_ref, bias_ref, gain_ref, xp_hbm, u_hbm, up_hbm, down_hbm,
    table_out, unit0_out, scale0_out, slope0_out, unit1_out, scale1_out, slope1_out, up_out,
    h0, h1, conv, norm, h2, up, xp_ref, u_ref, up_ref, down_ref,
    table_ref, unit0, scale0, slope0, unit1, scale1, slope1, lanes, sems, out_sems,
):
    fetch()
    low, high = pl.ds(0, 1), pl.ds(1, 1)
    early = copies(
        [(up_hbm.at[low], up_ref.at[low]), (down_hbm.at[low], down_ref.at[low])],
        sems.at[pl.ds(0, 2)],
    )
    _, _, half = table_ref.shape
    width = up.shape[2]
    tokens = h_ref.shape[0]
    patch_rows = tokens // half
    wide = (patch_rows + 2) * half
    ready()
    late = copies(
        [
            (u_hbm, u_ref),
            (up_hbm.at[high], up_ref.at[high]),
            (down_hbm.at[high], down_ref.at[high]),
            (xp_hbm, xp_ref),
        ],
        sems.at[pl.ds(2, 4)],
    )
    h0[0:HALO] = lo_ref[...].reshape(HALO, half, width)
    h0[HALO : HALO + patch_rows] = h_ref[...].reshape(patch_rows, half, width)
    h0[HALO + patch_rows :] = hi_ref[...].reshape(HALO, half, width)
    conv_norm_rows(
        patch_rows + 2, h0, 0, k_ref, bias_ref, gain_ref, conv, unit0, scale0, norm, half
    )

    def to_h1(start, out):
        h1[start // half : (start + out.shape[0]) // half] = out.reshape(-1, half, width)

    early[0].wait()
    early[1].wait()
    mlp_forward(0, norm, conv, slope0, up_ref, down_ref, to_h1, wide, 2 * half)
    sent = copies(
        [(unit0, unit0_out), (scale0, scale0_out), (slope0, slope0_out)], out_sems.at[pl.ds(0, 3)]
    )
    late[0].wait()
    fill_weights(up, u_ref, lanes)
    sent += copies([(up, up_out)], out_sems.at[pl.ds(7, 1)])
    conv_norm_rows(
        patch_rows, h1, 1, k_ref, bias_ref, gain_ref, conv, unit1, scale1, norm, half
    )

    def to_h2(start, out):
        h2[start : start + out.shape[0], :] = out

    late[1].wait()
    late[2].wait()
    mlp_forward(1, norm, conv, slope1, up_ref, down_ref, to_h2, tokens, 2 * half)
    sent += copies(
        [(unit1, unit1_out), (scale1, scale1_out), (slope1, slope1_out)], out_sems.at[pl.ds(3, 3)]
    )
    late[3].wait()
    for ab in range(4):
        part = mm_t(up[ab], h2[...])
        for i in range(patch_rows):
            at = ab * patch_rows + i
            mine = part[:, i * half : (i + 1) * half]
            table_ref[at] = (xp_ref[at].astype(F32) + mine).astype(BF16)
    return sent + copies([(table_ref, table_out)], out_sems.at[pl.ds(6, 1)])


def is_cell(key, high):
    return jnp.where(key == jnp.asarray(high, BF16), jnp.asarray(1, BF16), jnp.asarray(0, BF16))


def identity(size):
    row = lax.broadcasted_iota(jnp.int32, (size, size), 0)
    col = lax.broadcasted_iota(jnp.int32, (size, size), 1)
    return jnp.where(row == col, 1.0, 0.0).astype(BF16)


def radiance_kernel(
    fetch, ready, pay_ref, enc_ref, tab_ref, head_ref, hbias_ref, gain_ref,
    table_hbm, u_hbm, up_hbm, down_hbm, unit1_hbm, scale1_hbm, slope1_hbm,
    innov_ref, cg_ref, first_ref, last_ref, gradt_out, den_out,
    enc, enct, heads, headst, keys, gt, gcell, up, xf, den, inputs, pre, out, sums, slope,
    table_ref, up_ref, down_ref, unit1_ref, scale1_ref, slope1_ref, gradt_ref, sems, out_sems,
):
    fetch()
    (table_in,) = copies([(table_hbm, table_ref)], sems.at[pl.ds(0, 1)])
    chans, emu = enc_ref.shape
    nchan = tab_ref.shape[0]
    cell_blocks, padded, half = table_ref.shape
    blocks = pay_ref.shape[0]
    block = 2 * 128
    tokens, width = cg_ref.shape
    lon_rows, lat = den.shape[1:]
    patch_rows = lon_rows // 2
    one_at = round_up(chans, 8)
    tail = padded - heads.shape[1]
    shift = one_at - tail
    ready()
    zeros = jnp.zeros((one_at - chans, 128), BF16)
    eye = identity(padded)
    for k in range(emu // 128):
        cols = slice(k * 128, (k + 1) * 128)
        enc[k, 0:chans, :] = enc_ref[:, cols]
        enc[k, chans:one_at, :] = zeros
        enc[k, one_at : one_at + nchan, :] = tab_ref[:, cols]
        enc[k, one_at + nchan :, :] = jnp.zeros((padded - one_at - nchan, 128), BF16)
        heads[k, 0:shift, :] = jnp.zeros((shift, 128), BF16)
        heads[k, shift : shift + nchan, :] = head_ref[:, cols]
        heads[k, shift + nchan :, :] = jnp.zeros((heads.shape[1] - shift - nchan, 128), BF16)
    headst[...] = jnp.zeros_like(headst)
    for k in range(0, emu // 128, padded // 128):
        rows = slice(k * 128, k * 128 + padded)
        flip = mm_t(eye, wide_dot([enc[k + n] for n in range(padded // 128)])).astype(BF16)
        for n in range(padded // 128):
            enct[n, rows, :] = flip[:, n * 128 : (n + 1) * 128]
        flip = mm_t(eye, wide_dot([heads[k + n] for n in range(padded // 128)])).astype(F32)
        headst[rows, 0:nchan] = flip[:, shift : shift + nchan]
    rows = heads.shape[1]
    spot = lax.broadcasted_iota(jnp.int32, (rows, nchan), 0)
    lane = lax.broadcasted_iota(jnp.int32, (rows, nchan), 1)
    bias_row = jnp.broadcast_to(hbias_ref[...], (rows, nchan))
    bias_col = jnp.sum(jnp.where(spot == lane + shift, bias_row, 0.0), axis=1, keepdims=True)

    table_in.wait()
    fetched = copies(
        [
            (u_hbm, up),
            (up_hbm.at[pl.ds(1, 1)], up_ref),
            (down_hbm.at[pl.ds(1, 1)], down_ref),
            (unit1_hbm, unit1_ref),
            (scale1_hbm, scale1_ref),
            (slope1_hbm, slope1_ref),
        ],
        sems.at[pl.ds(1, 6)],
    )
    split = lat_split(lat)
    for lon in range(lon_rows):
        i, a = lon // 2, lon % 2
        both = wide_dot([table_ref[(2 * a + b) * patch_rows + i] for b in range(2)])
        put_lon_row(xf, lon, lon_rows, mm(both, split))
    for k in range(lat // 128):
        part = xf[k, 0 : chans * lon_rows, :].reshape(chans, lon_rows, 128)
        den[:, :, k * 128 : (k + 1) * 128] = part.astype(BF16)
    sent = copies([(den, den_out)], out_sems.at[pl.ds(0, 1)])

    def row_of(pay, kind):
        return wide_dot([pay[2 * kind : 2 * kind + 1], pay[2 * kind + 1 : 2 * kind + 2]])

    def one_hot_of(pay):
        chan = row_of(pay, 1).astype(jnp.int32)
        at = lax.broadcasted_iota(jnp.int32, (rows, block), 0)
        return jnp.where(at == chan + shift, 1.0, 0.0)

    def gather(p):
        pay = pay_ref[p]
        cell = row_of(pay, 0).astype(jnp.int32)
        high = (cell // half).astype(F32)
        low = cell % half
        at = lax.broadcasted_iota(jnp.int32, (half, block), 0)
        key = jnp.where(at == low, high, -1.0).astype(BF16)
        for n in range(2):
            keys[2 * p + n] = key[:, n * 128 : (n + 1) * 128]
        picks = jnp.concatenate([is_cell(key, k) for k in range(cell_blocks)], axis=0)
        columns = mm(wide_dot([table_ref[k] for k in range(cell_blocks)]), picks)
        one_hot = one_hot_of(pay)
        inputs[0:tail, :] = columns[:tail].astype(BF16)
        inputs[tail:, :] = (columns[tail:] + one_hot).astype(BF16)

    def first_layer(p):
        pre[...] = mm(wide_dot([enct[n] for n in range(padded // 128)]), inputs[...]).astype(GELU)
        for n in range(2):
            chan = pay_ref[p][2 + n : 3 + n].astype(jnp.int32)
            at = jnp.broadcast_to(chan, headst.shape)
            picked = jnp.take_along_axis(headst[...], at, axis=1, mode="promise_in_bounds")
            out[:, n * 128 : (n + 1) * 128] = picked

    def activate():
        chunk, group = 32, 4
        total = None
        for first in range(0, emu, chunk * group):
            terms = None
            for start in range(first, first + chunk * group, chunk):
                at = pl.ds(start, chunk)
                act, tilt = gelu_pair(pre[at, :])
                head = out[at, :].astype(GELU)
                slope[at, :] = (tilt * head).astype(BF16)
                terms = act * head if terms is None else terms + act * head
            terms = terms.astype(F32)
            total = terms if total is None else total + terms
        sums[...] = jnp.sum(total.reshape(chunk // 8, 8, block), axis=0)

    def finish(p):
        pay = pay_ref[p]
        bias = jnp.sum(bias_col * one_hot_of(pay), axis=0, keepdims=True)
        predicted = 0.5 * jnp.sum(sums[...], axis=0, keepdims=True) + bias
        innov = row_of(pay, 3) * (predicted - row_of(pay, 2))
        grad = mm(wide_dot([enc[k] for k in range(emu // 128)]), slope[...])
        grad = (grad * (0.5 * innov)).astype(BF16)
        for n in range(2):
            innov_ref[pl.ds(2 * p + n, 1), :] = innov[:, n * 128 : (n + 1) * 128]
            gt[2 * p + n] = grad[:, n * 128 : (n + 1) * 128]

    def step(p, least=0, most=4):
        if most > 3:
            finish(p - 3)
        if least < 3 <= most:
            activate()
        if least < 2 <= most:
            first_layer(p - 1)
        if least < 1:
            gather(p)

    for p in range(3):
        step(p, 0, p + 1)
    lax.fori_loop(3, blocks, lambda p, carry: (step(p), carry)[1], 0)
    for p in range(3):
        step(blocks + p, p + 1, 4)

    lane_blocks = keys.shape[0]

    count = 4

    def scatter(r, carry):
        key = wide_dot([keys[k] for k in range(lane_blocks)])
        high = (count * r).astype(F32)
        picks = []
        for n in range(count):
            want = jnp.full((1, 1), high + n, F32).astype(BF16)
            picks.append(jnp.where(key == want, jnp.asarray(1, BF16), jnp.asarray(0, BF16)))
        lhs = jnp.concatenate(picks, axis=0)
        total = mm_t(lhs, wide_dot([gt[k] for k in range(lane_blocks)])).astype(BF16)
        at = pl.ds(pl.multiple_of(r * count * half, count * half), count * half)
        for n in range(padded // 128):
            gcell[n, at, :] = total[:, n * 128 : (n + 1) * 128]
        return carry

    lax.fori_loop(0, cell_blocks // count, scatter, 0)
    for one in fetched:
        one.wait()
    flip = mm_t(eye, wide_dot([gcell[n] for n in range(padded // 128)])).astype(BF16)
    for k in range(cell_blocks):
        gradt_ref[k] = flip[:, k * half : (k + 1) * half]
    sent += copies([(gradt_ref, gradt_out)], out_sems.at[pl.ds(1, 1)])
    upstream = None
    for ab in range(4):
        at = slice(ab * tokens, (ab + 1) * tokens)
        part = mm(wide_dot([gcell[n, at, :] for n in range(padded // 128)]), up[ab])
        upstream = part if upstream is None else upstream + part
    grad = mlp_backward(
        upstream, unit1_ref[...].astype(F32), whole(scale1_ref[...], width), slope1_ref[...],
        0.5 * gain_ref[...].astype(F32)[1:2], up_ref[0], down_ref[0],
    ).astype(BF16)
    cg_ref[...] = grad
    first_ref[...] = grad[: HALO * half]
    last_ref[...] = grad[tokens - HALO * half :]
    return sent


def last_kernel(
    fetch, ready, cg_ref, lo_ref, hi_ref, k_ref, gain_ref,
    unit0_hbm, scale0_hbm, slope0_hbm, gradt_hbm, w_hbm, up_hbm, down_hbm, out_hbm,
    c1, up1, c0, bottom, full, xf, wp,
    unit0_ref, scale0_ref, slope0_ref, gradt_ref, up_ref, down_ref, sems, out_sems,
):
    fetch()
    wide, block = up1.shape[0], 2 * c1.shape[1]
    kept = [(slope0_hbm, slope0_ref), (unit0_hbm, unit0_ref), (scale0_hbm, scale0_ref)]
    early = copies(
        [(down_hbm.at[pl.ds(0, 1)], down_ref), (up_hbm.at[pl.ds(0, 1)], up_ref)], sems.at[pl.ds(0, 2)]
    )
    ready()
    pairs = []
    for start in range(0, wide, block):
        pairs += [(src.at[pl.ds(start, block)], dst.at[pl.ds(start, block)]) for src, dst in kept]
    late = copies(pairs + [(w_hbm, wp), (gradt_hbm, gradt_ref)], sems.at[pl.ds(2, len(pairs) + 2)])
    rows_out, lat = out_hbm.shape
    half = lat // 2
    padded, width = wp.shape[1:]
    tokens = cg_ref.shape[0]
    patch_rows = tokens // half
    lon_rows = 2 * patch_rows
    chans = rows_out // lon_rows
    c1[0:HALO] = lo_ref[...].reshape(HALO, half, width)
    c1[HALO : HALO + patch_rows] = cg_ref[...].reshape(patch_rows, half, width)
    c1[HALO + patch_rows :] = hi_ref[...].reshape(HALO, half, width)
    taps = load_taps(k_ref, 1, True)

    def row1(i, carry):
        at = pl.ds(pl.multiple_of(i * half, half), half)
        up1[at, :] = conv_row([c1[i + p].astype(F32) for p in range(3)], taps)
        return carry

    lax.fori_loop(0, patch_rows + 2, row1, 0)
    half_gain = 0.5 * gain_ref[...].astype(F32)[0:1]
    early[0].wait()
    early[1].wait()
    for start in range(0, wide, block):
        at = pl.ds(start, block)
        for n in range(3):
            late[start // block * 3 + n].wait()
        grad = mlp_backward(
            up1[at, :], unit0_ref[at, :].astype(F32), whole(scale0_ref[at, :], width),
            slope0_ref[at, :],
            half_gain, up_ref[0], down_ref[0],
        )
        c0[start // half : start // half + 2] = grad.astype(BF16).reshape(2, half, width)
    taps0 = load_taps(k_ref, 0, True)

    def row0(i, carry):
        at = pl.ds(pl.multiple_of(i * half, half), half)
        bottom[at, :] = conv_row([c0[i + p].astype(F32) for p in range(3)], taps0).astype(BF16)
        return carry

    lax.fori_loop(0, patch_rows, row0, 0)
    late[-2].wait()
    late[-1].wait()
    for ab in range(4):
        part = mm_t(wp[ab], bottom[...])
        for i in range(patch_rows):
            at = ab * patch_rows + i
            mine = part[:, i * half : (i + 1) * half]
            full[at] = (gradt_ref[at].astype(F32) + mine).astype(BF16)
    split = lat_split(lat)
    sent = []
    spans = [(0, padded // 2), (padded // 2, chans)]
    for n, (low, high) in enumerate(spans):
        for lon in range(lon_rows):
            i, a = lon // 2, lon % 2
            both = wide_dot([full[(2 * a + b) * patch_rows + i, low : low + padded // 2] for b in range(2)])
            put_lon_row(xf, lon, lon_rows, mm(both, split), low)
        at = pl.ds(low * lon_rows, (high - low) * lon_rows)
        sent += copies(
            [(xf.at[k, at, :], out_hbm.at[at, pl.ds(k * 128, 128)]) for k in range(lat // 128)],
            out_sems.at[pl.ds(n * (lat // 128), lat // 128)],
        )
    return sent


ANY = pl.BlockSpec(memory_space=pl.ANY)
IN_SMEM = pl.BlockSpec(memory_space=pltpu.SMEM)


def whole_copies(kernel, counts, *refs):
    parts, at = [], 0
    for count in counts:
        parts.append(refs[at : at + count])
        at += count
    smem, args, far, outs, far_outs, args_in, outs_in, scratch, arg_sems, out_sems = parts
    fetched = []

    def fetch():
        if args:
            fetched.extend(copies(list(zip(args, args_in)), arg_sems[0]))

    def ready():
        for one in fetched:
            one.wait()

    sent = kernel(fetch, ready, *smem, *args_in, *far, *outs_in, *far_outs, *scratch)
    if outs:
        sent = list(sent) + copies(list(zip(outs_in, outs)), out_sems[0])
    for one in sent:
        one.wait()


def call(kernel, outs, scratch, copies_in, copies_out, cost, smem=(), args=(), far=(), far_outs=()):
    sems = [pltpu.SemaphoreType.DMA((n,)) for n in (copies_in, copies_out) if n]
    own = [[pltpu.SemaphoreType.DMA((n,))] if n else [] for n in (len(args), len(outs))]
    counts = (
        len(smem), len(args), len(far), len(outs), len(far_outs), len(args), len(outs),
        len(scratch) + len(sems), len(own[0]), len(own[1]),
    )
    held = [(arg.shape, arg.dtype) for arg in args] + list(outs) + list(scratch)
    return pl.pallas_call(
        functools.partial(whole_copies, kernel, counts),
        out_shape=[jax.ShapeDtypeStruct(shape, dtype) for shape, dtype in (*outs, *far_outs)],
        in_specs=[IN_SMEM] * len(smem) + [ANY] * (len(args) + len(far)),
        out_specs=[ANY] * (len(outs) + len(far_outs)),
        scratch_shapes=[pltpu.VMEM(shape, dtype) for shape, dtype in held] + sems + own[0] + own[1],
        cost_estimate=pl.CostEstimate(
            flops=cost[0], bytes_accessed=cost[1], transcendentals=0
        ),
        compiler_params=pltpu.CompilerParams(vmem_limit_bytes=60 << 20),
    )(*smem, *args, *far)


def round_up(value, to):
    return -(-value // to) * to


BLOCK = 256


def shards(
    prior_state, patch_embed, conv_kernel, conv_bias, norm_gain, mlp_up, mlp_down, patch_unembed,
    emu_encode, chan_table, chan_head, head_bias, obs_cells, obs_chans, obs_values, obs_counts,
):
    lon_size = lax.axis_size("lon")
    lon_rows, chans, lat = prior_state.shape
    slots = obs_cells.shape[0]
    per_peer = slots // lon_size
    width = patch_embed.shape[3]
    hidden_size = mlp_up.shape[2]
    emu = emu_encode.shape[1]
    nchan = chan_table.shape[0]
    half, patch_rows = lat // 2, lon_rows // 2
    tokens, cells = half * patch_rows, lat * lon_rows
    wide = tokens + 2 * half
    head_pad = 32
    padded = round_up(chans + nchan, 256)
    packed = per_peer == BLOCK
    lanes = slots // 128
    state = jnp.transpose(prior_state, (1, 0, 2))
    u = jnp.transpose(patch_unembed, (1, 3, 2, 0))
    w = jnp.transpose(patch_embed, (0, 2, 1, 3))
    taps = jnp.transpose(conv_kernel, (1, 2, 0, 3))
    forward = [(i, (i + 1) % lon_size) for i in range(lon_size)]
    backward = [(target, source) for source, target in forward]

    halo = ((HALO * half, width), BF16)
    fat = ((wide, width), F32)
    fat_unit, thin_unit = ((wide, width), BF16), ((tokens, width), BF16)
    fat_scale, thin_scale = ((wide, 128), F32), ((tokens, 128), F32)
    fat_slope, thin_slope = ((wide, hidden_size), BF16), ((tokens, hidden_size), BF16)
    by_cell = ((cells // half, padded, half), BF16)
    rows_f32 = ((lat // 128, padded * lon_rows, 128), F32)
    maps = ((4, padded, width), BF16)
    lane_maps = ((width // 128, 2 * chans, 128), F32)
    maps_in = ((2, chans, 2, width), BF16)
    one_up, one_down = ((1, width, hidden_size), BF16), ((1, hidden_size, width), BF16)

    smem, args, outs = (), (), []
    if packed:
        smem = (obs_counts,)
        args = tuple(x.reshape(lanes, 128) for x in (obs_cells, obs_chans, obs_values))
        outs = [((lanes * 4, 128), F32)]
    hidden, first, last, *pay, xp, w = call(
        functools.partial(embed_kernel, lon_size if packed else None),
        [((tokens, width), BF16), halo, halo] + outs,
        [
            rows_f32, ((tokens, 4 * padded), BF16), maps, by_cell,
            ((chans, lon_rows, lat), BF16), maps_in, lane_maps,
        ],
        5, cells // half + 1, (2 * tokens * 12 * padded * width, 4 * state.size),
        smem, args, (state, w), (by_cell, maps),
    )
    low = lax.ppermute(last, "lon", forward)
    high = lax.ppermute(first, "lon", backward)
    if packed:
        sent = pay[0].reshape(lon_size, 4 * per_peer // 128, 128)
    else:
        tile_lon, tile_lat = obs_cells // lat, obs_cells % lat
        place = (tile_lon % 2 * 2 + tile_lat % 2) * patch_rows + tile_lon // 2
        place = place * half + tile_lat // 2
        live = (jnp.arange(slots, dtype=jnp.int32) < obs_counts[0]).astype(F32)
        sent = jnp.stack(
            [
                part.astype(F32).reshape(lon_size, per_peer)
                for part in (place, obs_chans, obs_values, live)
            ],
            axis=1,
        )
    pay = lax.all_to_all(sent, "lon", split_axis=0, concat_axis=0, tiled=True)
    if not packed:
        group = BLOCK // per_peer
        pay = pay.reshape(lon_size // group, group, 4, per_peer)
        pay = jnp.transpose(pay, (0, 2, 1, 3)).reshape(lon_size // group, 8, 128)
    table, unit0, scale0, slope0, unit1, scale1, slope1, u = call(
        forward_kernel,
        [],
        [
            ((patch_rows + 2 * HALO, half, width), BF16),
            ((patch_rows + 2, half, width), BF16),
            fat,
            ((wide, width), BF16),
            ((tokens, width), BF16),
            maps, by_cell, maps_in,
            (mlp_up.shape, BF16), (mlp_down.shape, BF16),
            by_cell, fat_unit, fat_scale, fat_slope, thin_unit, thin_scale, thin_slope,
            lane_maps,
        ],
        6, 8, (3 * 10**9, 10**7),
        (), (hidden, low, high, taps, conv_bias, norm_gain), (xp, u, mlp_up, mlp_down),
        (by_cell, fat_unit, fat_scale, fat_slope, thin_unit, thin_scale, thin_slope, maps),
    )
    innov, grad, first, last, grad_t, denoised = call(
        radiance_kernel,
        [((lanes, 128), F32), ((tokens, width), BF16), halo, halo],
        [
            ((emu // 128, padded, 128), BF16),
            ((padded // 128, emu, 128), BF16),
            ((emu // 128, head_pad, 128), BF16),
            ((emu, 128), F32),
            ((lanes, half, 128), BF16),
            ((lanes, padded, 128), BF16),
            ((padded // 128, cells, 128), BF16),
            maps, rows_f32, ((chans, lon_rows, lat), BF16),
            ((padded, BLOCK), BF16), ((emu, BLOCK), GELU), ((emu, BLOCK), F32),
            ((8, BLOCK), F32), ((emu, BLOCK), BF16),
            by_cell, one_up, one_down, thin_unit, thin_scale, thin_slope, by_cell,
        ],
        7, 2, (14 * 10**9, 10**7),
        (),
        (pay, emu_encode, chan_table, chan_head, head_bias.reshape(1, nchan), norm_gain),
        (table, u, mlp_up, mlp_down, unit1, scale1, slope1),
        (by_cell, ((chans, lon_rows, lat), BF16)),
    )
    back = lax.ppermute(last, "lon", forward)
    ahead = lax.ppermute(first, "lon", backward)
    if packed:
        innov = innov.reshape(lon_size, per_peer // 128, 128)
    else:
        innov = innov.reshape(lon_size, per_peer)
    innovations = lax.all_to_all(innov, "lon", split_axis=0, concat_axis=0, tiled=True)
    (out,) = call(
        last_kernel,
        [],
        [
            ((patch_rows + 2 * HALO, half, width), BF16),
            fat,
            ((patch_rows + 2, half, width), BF16),
            ((tokens, width), BF16),
            by_cell, rows_f32, maps,
            fat_unit, fat_scale, fat_slope, by_cell, one_up, one_down,
        ],
        4 + 3 * (patch_rows + 2) // 2, 2 * (lat // 128), (4 * 10**9, 10**7),
        (), (grad, back, ahead, taps, norm_gain),
        (unit0, scale0, slope0, grad_t, w, mlp_up, mlp_down),
        (((chans * lon_rows, lat), F32),),
    )
    state_gradient = jnp.transpose(out.reshape(chans, lon_rows, lat), (1, 0, 2))
    return (jnp.transpose(denoised, (1, 0, 2)), state_gradient, innovations.reshape(slots))


def solution(mesh):
    split = P(("groups", "lon"))
    placed = (split,) + (P(),) * 11 + (split,) * 4
    return jax.shard_map(
        shards, mesh=mesh, in_specs=placed, out_specs=(split,) * 3, check_vma=False
    )
```

```python
import functools

import jax
import jax.numpy as jnp
from jax import lax
from jax.experimental import pallas as pl
from jax.experimental.pallas import tpu as pltpu
from jax.sharding import PartitionSpec as P


HALO = 2

root_coef = 0.7978845608028654
cubic_coef = 0.044715
norm_eps = 1e-06

F32 = jnp.float32
BF16 = jnp.bfloat16
GELU = jnp.bfloat16


def mm(a, b):
    return lax.dot_general(a, b, (((1,), (0,)), ((), ())), preferred_element_type=F32)


def mm_t(a, b):
    return lax.dot_general(a, b, (((1,), (1,)), ((), ())), preferred_element_type=F32)


def gelu_pair(v):
    v = v.astype(GELU)
    one = jnp.asarray(1.0, GELU)
    sq = v * v
    cube = jnp.asarray(root_coef * cubic_coef, GELU) * sq
    inner = v * (jnp.asarray(root_coef, GELU) + cube)
    tangent = jnp.tanh(inner)
    upper = one + tangent
    poly = jnp.asarray(root_coef, GELU) + jnp.asarray(3 * root_coef * cubic_coef, GELU) * sq
    slope = upper * (one + v * poly * (one - tangent))
    return v * upper, slope


def copies(pairs, sems):
    started = [pltpu.make_async_copy(src, dst, sems.at[n]) for n, (src, dst) in enumerate(pairs)]
    for one in started:
        one.start()
    return started


def wide_dot(parts):
    return jnp.concatenate(parts, axis=1)


def lat_split(size, dtype=BF16):
    row = lax.broadcasted_iota(jnp.int32, (size, size), 0)
    col = lax.broadcasted_iota(jnp.int32, (size, size), 1)
    half = size // 2
    want = jnp.where(row < half, 2 * row, 2 * (row - half) + 1)
    return jnp.where(col == want, 1.0, 0.0).astype(dtype)


def shift_rows(x, by):
    rows = x.shape[0]
    at = lax.broadcasted_iota(jnp.int32, x.shape, 0)
    if by == 1:
        return jnp.where(at == 0, 0.0, pltpu.roll(x, 1, 0))
    return jnp.where(at == rows - 1, 0.0, pltpu.roll(x, rows - 1, 0))


def conv_row(rows, taps):
    sums = []
    for q in range(3):
        total = taps[0][q] * rows[0]
        for p in (1, 2):
            total = total + taps[p][q] * rows[p]
        sums.append(total)
    return sums[1] + shift_rows(sums[0], 1) + shift_rows(sums[2], -1)


def load_taps(k_ref, layer, flip):
    def one(p, q):
        if flip:
            p, q = 2 - p, 2 - q
        return k_ref[p, q, :, :].astype(F32)[layer : layer + 1]

    return [[one(p, q) for q in range(3)] for p in range(3)]


def whole(x, width):
    return jnp.concatenate([x] * (width // 128), axis=1)


def row_mean(x):
    width = x.shape[-1]
    return mm(x.astype(BF16), jnp.full((width, width), 1.0 / width, BF16))


def fill_lanes(xf, x, first, chans, lon_rows):
    for k in range(xf.shape[0]):
        part = x[first : first + chans, :, k * 128 : (k + 1) * 128].astype(F32)
        xf[k, first * lon_rows : (first + chans) * lon_rows, :] = part.reshape(chans * lon_rows, 128)


def lon_row(xf, lon, lon_rows):
    count = xf.shape[1] // lon_rows
    parts = [xf[k, pl.ds(lon, count, stride=lon_rows), :] for k in range(xf.shape[0])]
    return jnp.concatenate(parts, axis=1)


def put_lon_row(xf, lon, lon_rows, value, first=0):
    for k in range(xf.shape[0]):
        at = pl.ds(first * lon_rows + lon, value.shape[0], stride=lon_rows)
        xf[k, at, :] = value[:, k * 128 : (k + 1) * 128]


def fill_weights(out, w_ref, lanes):
    chans = w_ref.shape[1]
    for a in range(2):
        for k in range(out.shape[2] // 128):
            cols = slice(k * 128, (k + 1) * 128)
            lanes[k] = w_ref[a, :, :, cols].astype(F32).reshape(2 * chans, 128)
            for b in range(2):
                rows = lanes[k, pl.ds(b, chans, stride=2), :]
                out[2 * a + b, 0:chans, cols] = rows.astype(BF16)
    for ab in range(4):
        out[ab, chans:, :] = jnp.zeros((out.shape[1] - chans, out.shape[2]), BF16)


def embed_kernel(peers, fetch, ready, *refs):
    packed = peers is not None
    if packed:
        count_ref, cells_ref, chans_ref, values_ref, x_hbm, w_hbm = refs[:6]
        h_ref, first_ref, last_ref, pay_ref, xp_out, wp_out, *scratch = refs[6:]
    else:
        x_hbm, w_hbm, h_ref, first_ref, last_ref, xp_out, wp_out, *scratch = refs
    xf, tcat, wp, xp_ref, x_ref, w_ref, lanes, in_sems, sems = scratch
    chans, lon_rows, lat = x_ref.shape
    padded, width = wp.shape[1:]
    half = lat // 2
    edges = [chans * n // 4 for n in range(5)]
    spans = [pl.ds(lo, hi - lo) for lo, hi in zip(edges, edges[1:])]
    fetched = copies([(x_hbm.at[at], x_ref.at[at]) for at in spans] + [(w_hbm, w_ref)], in_sems)
    fetch()
    for k in range(lat // 128):
        xf[k, chans * lon_rows :, :] = jnp.zeros(((padded - chans) * lon_rows, 128), F32)
    for n in range(4):
        fetched[n].wait()
        fill_lanes(xf, x_ref, edges[n], edges[n + 1] - edges[n], lon_rows)
    split = lat_split(lat)
    sent = []
    for lon in range(lon_rows):
        i, a = lon // 2, lon % 2
        rows = lon_row(xf, lon, lon_rows).astype(BF16)
        tokens = mm_t(split, rows).astype(BF16)
        part = mm_t(rows, split).astype(BF16)
        for b in range(2):
            place = (2 * a + b) * (lon_rows // 2) + i
            xp_ref[place] = part[:, b * half : (b + 1) * half]
            here = pl.ds(place, 1)
            sent += copies([(xp_ref.at[here], xp_out.at[here])], sems.at[here])
            tcat[i * half : (i + 1) * half, (2 * a + b) * padded : (2 * a + b + 1) * padded] = tokens[
                b * half : (b + 1) * half
            ]
    fetched[4].wait()
    fill_weights(wp, w_ref, lanes)
    sent += copies([(wp, wp_out)], sems.at[pl.ds(2 * lon_rows, 1)])
    hidden = mm(tcat[...], wp[...].reshape(4 * padded, width)).astype(BF16)
    h_ref[...] = hidden
    first_ref[...] = hidden[: HALO * half]
    last_ref[...] = hidden[hidden.shape[0] - HALO * half :]
    ready()
    if not packed:
        return sent
    rows, wide = cells_ref.shape
    per = rows // peers
    for part in range(per):
        at = pl.ds(part, peers, stride=per)
        cell = cells_ref[at, :]
        tile_lon, tile_lat = cell // lat, cell % lat
        place = (
            (tile_lon % 2 * 2 + tile_lat % 2) * (lon_rows // 2) + tile_lon // 2
        ) * half + tile_lat // 2
        slot = (
            lax.broadcasted_iota(jnp.int32, (peers, wide), 0) * (per * wide)
            + part * wide
            + lax.broadcasted_iota(jnp.int32, (peers, wide), 1)
        )
        live = jnp.where(slot < count_ref[0], 1.0, 0.0)
        kinds = (place.astype(F32), chans_ref[at, :].astype(F32), values_ref[at, :], live)
        for kind, value in enumerate(kinds):
            pay_ref[pl.ds(kind * per + part, peers, stride=4 * per), :] = value
    return sent


def mlp_forward(layer, norm, conv, slope, up_ref, down_ref, store, tokens, block):
    for start in range(0, tokens, block):
        rows = pl.ds(start, block)
        value, tilt = gelu_pair(mm(norm[rows, :], up_ref[layer]))
        slope[rows, :] = tilt.astype(BF16)
        out = conv[rows, :] + 0.5 * mm(value.astype(BF16), down_ref[layer])
        store(start, out.astype(BF16))


def conv_norm_rows(count, source, layer, k_ref, bias_ref, gain_ref, conv, unit, scale, norm, half):
    taps = load_taps(k_ref, layer, False)
    bias = bias_ref[...].astype(F32)[layer : layer + 1]
    gain = gain_ref[...].astype(F32)[layer : layer + 1]

    def row(i, carry):
        out = conv_row([source[i + p].astype(F32) for p in range(3)], taps) + bias
        inv = lax.rsqrt(row_mean(out * out) + norm_eps)
        at = pl.ds(pl.multiple_of(i * half, half), half)
        u = out * inv
        conv[at, :] = out
        unit[at, :] = u.astype(BF16)
        scale[at, :] = inv[:, 0:128]
        norm[at, :] = (u * gain).astype(BF16)
        return carry

    lax.fori_loop(0, count, row, 0, unroll=True)


def mlp_backward(upstream, unit, scale, slope, half_gain, up, down):
    pre = (mm_t(upstream.astype(BF16), down) * slope.astype(F32)).astype(BF16)
    scaled = mm_t(pre, up) * half_gain
    return upstream + scale * (scaled - unit * row_mean(scaled * unit))


def forward_kernel(
    fetch, ready, h_ref, lo_ref, hi_ref, k_ref, bias_ref, gain_ref, xp_hbm, u_hbm, up_hbm, down_hbm,
    table_out, unit0_out, scale0_out, slope0_out, unit1_out, scale1_out, slope1_out, up_out,
    h0, h1, conv, norm, h2, up, xp_ref, u_ref, up_ref, down_ref,
    table_ref, unit0, scale0, slope0, unit1, scale1, slope1, lanes, sems, out_sems,
):
    fetch()
    low, high = pl.ds(0, 1), pl.ds(1, 1)
    early = copies(
        [(up_hbm.at[low], up_ref.at[low]), (down_hbm.at[low], down_ref.at[low])],
        sems.at[pl.ds(0, 2)],
    )
    _, _, half = table_ref.shape
    width = up.shape[2]
    tokens = h_ref.shape[0]
    patch_rows = tokens // half
    wide = (patch_rows + 2) * half
    ready()
    late = copies(
        [
            (u_hbm, u_ref),
            (up_hbm.at[high], up_ref.at[high]),
            (down_hbm.at[high], down_ref.at[high]),
            (xp_hbm, xp_ref),
        ],
        sems.at[pl.ds(2, 4)],
    )
    h0[0:HALO] = lo_ref[...].reshape(HALO, half, width)
    h0[HALO : HALO + patch_rows] = h_ref[...].reshape(patch_rows, half, width)
    h0[HALO + patch_rows :] = hi_ref[...].reshape(HALO, half, width)
    conv_norm_rows(
        patch_rows + 2, h0, 0, k_ref, bias_ref, gain_ref, conv, unit0, scale0, norm, half
    )

    def to_h1(start, out):
        h1[start // half : (start + out.shape[0]) // half] = out.reshape(-1, half, width)

    early[0].wait()
    early[1].wait()
    mlp_forward(0, norm, conv, slope0, up_ref, down_ref, to_h1, wide, 2 * half)
    sent = copies(
        [(unit0, unit0_out), (scale0, scale0_out), (slope0, slope0_out)], out_sems.at[pl.ds(0, 3)]
    )
    late[0].wait()
    fill_weights(up, u_ref, lanes)
    sent += copies([(up, up_out)], out_sems.at[pl.ds(6, 1)])
    conv_norm_rows(
        patch_rows, h1, 1, k_ref, bias_ref, gain_ref, conv, unit1, scale1, norm, half
    )

    def to_h2(start, out):
        h2[start : start + out.shape[0], :] = out

    late[1].wait()
    late[2].wait()
    mlp_forward(1, norm, conv, slope1, up_ref, down_ref, to_h2, tokens, 2 * half)
    sent += copies(
        [(unit1, unit1_out), (scale1, scale1_out), (slope1, slope1_out)], out_sems.at[pl.ds(3, 3)]
    )
    late[3].wait()
    for ab in range(4):
        part = mm_t(up[ab], h2[...])
        here = pl.ds(ab * patch_rows, patch_rows)
        for i in range(patch_rows):
            at = ab * patch_rows + i
            mine = part[:, i * half : (i + 1) * half]
            table_ref[at] = (xp_ref[at].astype(F32) + mine).astype(BF16)
        sent += copies([(table_ref.at[here], table_out.at[here])], out_sems.at[pl.ds(7 + ab, 1)])
    return sent


def is_cell(key, high):
    return jnp.where(key == jnp.asarray(high, BF16), jnp.asarray(1, BF16), jnp.asarray(0, BF16))


def identity(size):
    row = lax.broadcasted_iota(jnp.int32, (size, size), 0)
    col = lax.broadcasted_iota(jnp.int32, (size, size), 1)
    return jnp.where(row == col, 1.0, 0.0).astype(BF16)


def radiance_kernel(
    fetch, ready, pay_ref, enc_ref, tab_ref, head_ref, hbias_ref, gain_ref,
    table_hbm, u_hbm, up_hbm, down_hbm, unit1_hbm, scale1_hbm, slope1_hbm,
    innov_ref, cg_ref, first_ref, last_ref, gradt_out, den_out,
    enc, enct, heads, headst, keys, gt, gcell, up, xf, den, inputs, pre, out, sums, slope,
    table_ref, up_ref, down_ref, unit1_ref, scale1_ref, slope1_ref, gradt_ref, sems, out_sems,
):
    fetch()
    (table_in,) = copies([(table_hbm, table_ref)], sems.at[pl.ds(0, 1)])
    chans, emu = enc_ref.shape
    nchan = tab_ref.shape[0]
    cell_blocks, padded, half = table_ref.shape
    blocks = pay_ref.shape[0]
    block = 2 * 128
    tokens, width = cg_ref.shape
    lon_rows, lat = den.shape[1:]
    patch_rows = lon_rows // 2
    one_at = round_up(chans, 8)
    tail = padded - heads.shape[1]
    shift = one_at - tail
    ready()
    zeros = jnp.zeros((one_at - chans, 128), BF16)
    eye = identity(padded)
    for k in range(emu // 128):
        cols = slice(k * 128, (k + 1) * 128)
        enc[k, 0:chans, :] = enc_ref[:, cols]
        enc[k, chans:one_at, :] = zeros
        enc[k, one_at : one_at + nchan, :] = tab_ref[:, cols]
        enc[k, one_at + nchan :, :] = jnp.zeros((padded - one_at - nchan, 128), BF16)
        heads[k, 0:shift, :] = jnp.zeros((shift, 128), BF16)
        heads[k, shift : shift + nchan, :] = head_ref[:, cols]
        heads[k, shift + nchan :, :] = jnp.zeros((heads.shape[1] - shift - nchan, 128), BF16)
    headst[...] = jnp.zeros_like(headst)
    for k in range(0, emu // 128, padded // 128):
        rows = slice(k * 128, k * 128 + padded)
        flip = mm_t(eye, wide_dot([enc[k + n] for n in range(padded // 128)])).astype(BF16)
        for n in range(padded // 128):
            enct[n, rows, :] = flip[:, n * 128 : (n + 1) * 128]
        flip = mm_t(eye, wide_dot([heads[k + n] for n in range(padded // 128)])).astype(F32)
        headst[rows, 0:nchan] = flip[:, shift : shift + nchan]
    rows = heads.shape[1]
    spot = lax.broadcasted_iota(jnp.int32, (rows, nchan), 0)
    lane = lax.broadcasted_iota(jnp.int32, (rows, nchan), 1)
    bias_row = jnp.broadcast_to(hbias_ref[...], (rows, nchan))
    bias_col = jnp.sum(jnp.where(spot == lane + shift, bias_row, 0.0), axis=1, keepdims=True)

    table_in.wait()
    fetched = copies(
        [
            (u_hbm, up),
            (up_hbm.at[pl.ds(1, 1)], up_ref),
            (down_hbm.at[pl.ds(1, 1)], down_ref),
            (unit1_hbm, unit1_ref),
            (scale1_hbm, scale1_ref),
            (slope1_hbm, slope1_ref),
        ],
        sems.at[pl.ds(1, 6)],
    )

    def row_of(pay, kind):
        return wide_dot([pay[2 * kind : 2 * kind + 1], pay[2 * kind + 1 : 2 * kind + 2]])

    def one_hot_of(pay):
        chan = row_of(pay, 1).astype(jnp.int32)
        at = lax.broadcasted_iota(jnp.int32, (rows, block), 0)
        return jnp.where(at == chan + shift, 1.0, 0.0)

    def gather(p):
        pay = pay_ref[p]
        cell = row_of(pay, 0).astype(jnp.int32)
        high = (cell // half).astype(F32)
        low = cell % half
        at = lax.broadcasted_iota(jnp.int32, (half, block), 0)
        key = jnp.where(at == low, high, -1.0).astype(BF16)
        for n in range(2):
            keys[2 * p + n] = key[:, n * 128 : (n + 1) * 128]
        picks = jnp.concatenate([is_cell(key, k) for k in range(cell_blocks)], axis=0)
        columns = mm(wide_dot([table_ref[k] for k in range(cell_blocks)]), picks)
        one_hot = one_hot_of(pay)
        inputs[0:tail, :] = columns[:tail].astype(BF16)
        inputs[tail:, :] = (columns[tail:] + one_hot).astype(BF16)

    def first_layer(p):
        pre[...] = mm(wide_dot([enct[n] for n in range(padded // 128)]), inputs[...]).astype(GELU)
        for n in range(2):
            chan = pay_ref[p][2 + n : 3 + n].astype(jnp.int32)
            at = jnp.broadcast_to(chan, headst.shape)
            picked = jnp.take_along_axis(headst[...], at, axis=1, mode="promise_in_bounds")
            out[:, n * 128 : (n + 1) * 128] = picked

    def activate():
        chunk, group = 32, 4
        total = None
        for first in range(0, emu, chunk * group):
            terms = None
            for start in range(first, first + chunk * group, chunk):
                at = pl.ds(start, chunk)
                act, tilt = gelu_pair(pre[at, :])
                head = out[at, :].astype(GELU)
                slope[at, :] = (tilt * head).astype(BF16)
                terms = act * head if terms is None else terms + act * head
            terms = terms.astype(F32)
            total = terms if total is None else total + terms
        sums[...] = jnp.sum(total.reshape(chunk // 8, 8, block), axis=0)

    def finish(p):
        pay = pay_ref[p]
        bias = jnp.sum(bias_col * one_hot_of(pay), axis=0, keepdims=True)
        predicted = 0.5 * jnp.sum(sums[...], axis=0, keepdims=True) + bias
        innov = row_of(pay, 3) * (predicted - row_of(pay, 2))
        grad = mm(wide_dot([enc[k] for k in range(emu // 128)]), slope[...])
        grad = (grad * (0.5 * innov)).astype(BF16)
        for n in range(2):
            innov_ref[pl.ds(2 * p + n, 1), :] = innov[:, n * 128 : (n + 1) * 128]
            gt[2 * p + n] = grad[:, n * 128 : (n + 1) * 128]

    def step(p, least=0, most=4):
        if most > 3:
            finish(p - 3)
        if least < 3 <= most:
            activate()
        if least < 2 <= most:
            first_layer(p - 1)
        if least < 1:
            gather(p)

    for p in range(3):
        step(p, 0, p + 1)
    lax.fori_loop(3, blocks, lambda p, carry: (step(p), carry)[1], 0)
    split = lat_split(lat)
    for lon in range(lon_rows):
        i, a = lon // 2, lon % 2
        both = wide_dot([table_ref[(2 * a + b) * patch_rows + i] for b in range(2)])
        put_lon_row(xf, lon, lon_rows, mm(both, split))
    for k in range(lat // 128):
        part = xf[k, 0 : chans * lon_rows, :].reshape(chans, lon_rows, 128)
        den[:, :, k * 128 : (k + 1) * 128] = part.astype(BF16)
    sent = copies([(den, den_out)], out_sems.at[pl.ds(0, 1)])
    for p in range(3):
        step(blocks + p, p + 1, 4)

    lane_blocks = keys.shape[0]

    count = 8

    def scatter(r, carry):
        key = wide_dot([keys[k] for k in range(lane_blocks)])
        high = (count * r).astype(F32)
        picks = []
        for n in range(count):
            want = jnp.full((1, 1), high + n, F32).astype(BF16)
            picks.append(jnp.where(key == want, jnp.asarray(1, BF16), jnp.asarray(0, BF16)))
        lhs = jnp.concatenate(picks, axis=0)
        total = mm_t(lhs, wide_dot([gt[k] for k in range(lane_blocks)])).astype(BF16)
        at = pl.ds(pl.multiple_of(r * count * half, count * half), count * half)
        for n in range(padded // 128):
            gcell[n, at, :] = total[:, n * 128 : (n + 1) * 128]
        return carry

    lax.fori_loop(0, cell_blocks // count, scatter, 0)
    for one in fetched:
        one.wait()
    flip = mm_t(eye, wide_dot([gcell[n] for n in range(padded // 128)])).astype(BF16)
    for k in range(cell_blocks):
        gradt_ref[k] = flip[:, k * half : (k + 1) * half]
    sent += copies([(gradt_ref, gradt_out)], out_sems.at[pl.ds(1, 1)])
    upstream = None
    for ab in range(4):
        at = slice(ab * tokens, (ab + 1) * tokens)
        part = mm(wide_dot([gcell[n, at, :] for n in range(padded // 128)]), up[ab])
        upstream = part if upstream is None else upstream + part
    grad = mlp_backward(
        upstream, unit1_ref[...].astype(F32), whole(scale1_ref[...], width), slope1_ref[...],
        0.5 * gain_ref[...].astype(F32)[1:2], up_ref[0], down_ref[0],
    ).astype(BF16)
    cg_ref[...] = grad
    first_ref[...] = grad[: HALO * half]
    last_ref[...] = grad[tokens - HALO * half :]
    return sent


def last_kernel(
    fetch, ready, cg_ref, lo_ref, hi_ref, k_ref, gain_ref,
    unit0_hbm, scale0_hbm, slope0_hbm, gradt_hbm, w_hbm, up_hbm, down_hbm, out_hbm,
    c1, up1, c0, bottom, full, xf, wp,
    unit0_ref, scale0_ref, slope0_ref, gradt_ref, up_ref, down_ref, sems, out_sems,
):
    fetch()
    wide, block = up1.shape[0], 2 * c1.shape[1]
    kept = [(slope0_hbm, slope0_ref), (unit0_hbm, unit0_ref), (scale0_hbm, scale0_ref)]
    early = copies(
        [(down_hbm.at[pl.ds(0, 1)], down_ref), (up_hbm.at[pl.ds(0, 1)], up_ref)], sems.at[pl.ds(0, 2)]
    )
    ready()
    pairs = []
    for start in range(0, wide, block):
        pairs += [(src.at[pl.ds(start, block)], dst.at[pl.ds(start, block)]) for src, dst in kept]
    late = copies(pairs + [(w_hbm, wp), (gradt_hbm, gradt_ref)], sems.at[pl.ds(2, len(pairs) + 2)])
    rows_out, lat = out_hbm.shape
    half = lat // 2
    padded, width = wp.shape[1:]
    tokens = cg_ref.shape[0]
    patch_rows = tokens // half
    lon_rows = 2 * patch_rows
    chans = rows_out // lon_rows
    c1[0:HALO] = lo_ref[...].reshape(HALO, half, width)
    c1[HALO : HALO + patch_rows] = cg_ref[...].reshape(patch_rows, half, width)
    c1[HALO + patch_rows :] = hi_ref[...].reshape(HALO, half, width)
    taps = load_taps(k_ref, 1, True)

    def row1(i, carry):
        at = pl.ds(pl.multiple_of(i * half, half), half)
        up1[at, :] = conv_row([c1[i + p].astype(F32) for p in range(3)], taps)
        return carry

    lax.fori_loop(0, patch_rows + 2, row1, 0, unroll=True)
    half_gain = 0.5 * gain_ref[...].astype(F32)[0:1]
    early[0].wait()
    early[1].wait()
    for start in range(0, wide, block):
        at = pl.ds(start, block)
        for n in range(3):
            late[start // block * 3 + n].wait()
        grad = mlp_backward(
            up1[at, :], unit0_ref[at, :].astype(F32), whole(scale0_ref[at, :], width),
            slope0_ref[at, :],
            half_gain, up_ref[0], down_ref[0],
        )
        c0[start // half : start // half + 2] = grad.astype(BF16).reshape(2, half, width)
    taps0 = load_taps(k_ref, 0, True)

    def row0(i, carry):
        at = pl.ds(pl.multiple_of(i * half, half), half)
        bottom[at, :] = conv_row([c0[i + p].astype(F32) for p in range(3)], taps0).astype(BF16)
        return carry

    lax.fori_loop(0, patch_rows, row0, 0, unroll=True)
    late[-2].wait()
    late[-1].wait()
    for ab in range(4):
        part = mm_t(wp[ab], bottom[...])
        for i in range(patch_rows):
            at = ab * patch_rows + i
            mine = part[:, i * half : (i + 1) * half]
            full[at] = (gradt_ref[at].astype(F32) + mine).astype(BF16)
    split = lat_split(lat)
    sent = []
    spans = [(0, padded // 2), (padded // 2, chans)]
    for n, (low, high) in enumerate(spans):
        for lon in range(lon_rows):
            i, a = lon // 2, lon % 2
            both = wide_dot([full[(2 * a + b) * patch_rows + i, low : low + padded // 2] for b in range(2)])
            put_lon_row(xf, lon, lon_rows, mm(both, split), low)
        at = pl.ds(low * lon_rows, (high - low) * lon_rows)
        sent += copies(
            [(xf.at[k, at, :], out_hbm.at[at, pl.ds(k * 128, 128)]) for k in range(lat // 128)],
            out_sems.at[pl.ds(n * (lat // 128), lat // 128)],
        )
    return sent


ANY = pl.BlockSpec(memory_space=pl.ANY)
IN_SMEM = pl.BlockSpec(memory_space=pltpu.SMEM)


def whole_copies(kernel, counts, *refs):
    parts, at = [], 0
    for count in counts:
        parts.append(refs[at : at + count])
        at += count
    smem, args, far, outs, far_outs, args_in, outs_in, scratch, arg_sems, out_sems = parts
    fetched = []

    def fetch():
        if args:
            fetched.extend(copies(list(zip(args, args_in)), arg_sems[0]))

    def ready():
        for one in fetched:
            one.wait()

    sent = kernel(fetch, ready, *smem, *args_in, *far, *outs_in, *far_outs, *scratch)
    if outs:
        sent = list(sent) + copies(list(zip(outs_in, outs)), out_sems[0])
    for one in sent:
        one.wait()


def call(kernel, outs, scratch, copies_in, copies_out, cost, smem=(), args=(), far=(), far_outs=()):
    sems = [pltpu.SemaphoreType.DMA((n,)) for n in (copies_in, copies_out) if n]
    own = [[pltpu.SemaphoreType.DMA((n,))] if n else [] for n in (len(args), len(outs))]
    counts = (
        len(smem), len(args), len(far), len(outs), len(far_outs), len(args), len(outs),
        len(scratch) + len(sems), len(own[0]), len(own[1]),
    )
    held = [(arg.shape, arg.dtype) for arg in args] + list(outs) + list(scratch)
    return pl.pallas_call(
        functools.partial(whole_copies, kernel, counts),
        out_shape=[jax.ShapeDtypeStruct(shape, dtype) for shape, dtype in (*outs, *far_outs)],
        in_specs=[IN_SMEM] * len(smem) + [ANY] * (len(args) + len(far)),
        out_specs=[ANY] * (len(outs) + len(far_outs)),
        scratch_shapes=[pltpu.VMEM(shape, dtype) for shape, dtype in held] + sems + own[0] + own[1],
        cost_estimate=pl.CostEstimate(
            flops=cost[0], bytes_accessed=cost[1], transcendentals=0
        ),
        compiler_params=pltpu.CompilerParams(vmem_limit_bytes=60 << 20),
    )(*smem, *args, *far)


def round_up(value, to):
    return -(-value // to) * to


BLOCK = 256


def shards(
    prior_state, patch_embed, conv_kernel, conv_bias, norm_gain, mlp_up, mlp_down, patch_unembed,
    emu_encode, chan_table, chan_head, head_bias, obs_cells, obs_chans, obs_values, obs_counts,
):
    lon_size = lax.axis_size("lon")
    lon_rows, chans, lat = prior_state.shape
    slots = obs_cells.shape[0]
    per_peer = slots // lon_size
    width = patch_embed.shape[3]
    hidden_size = mlp_up.shape[2]
    emu = emu_encode.shape[1]
    nchan = chan_table.shape[0]
    half, patch_rows = lat // 2, lon_rows // 2
    tokens, cells = half * patch_rows, lat * lon_rows
    wide = tokens + 2 * half
    head_pad = 32
    padded = round_up(chans + nchan, 256)
    packed = per_peer == BLOCK
    lanes = slots // 128
    state = jnp.transpose(prior_state, (1, 0, 2))
    u = jnp.transpose(patch_unembed, (1, 3, 2, 0))
    w = jnp.transpose(patch_embed, (0, 2, 1, 3))
    taps = jnp.transpose(conv_kernel, (1, 2, 0, 3))
    forward = [(i, (i + 1) % lon_size) for i in range(lon_size)]
    backward = [(target, source) for source, target in forward]

    halo = ((HALO * half, width), BF16)
    fat = ((wide, width), F32)
    fat_unit, thin_unit = ((wide, width), BF16), ((tokens, width), BF16)
    fat_scale, thin_scale = ((wide, 128), F32), ((tokens, 128), F32)
    fat_slope, thin_slope = ((wide, hidden_size), BF16), ((tokens, hidden_size), BF16)
    by_cell = ((cells // half, padded, half), BF16)
    rows_f32 = ((lat // 128, padded * lon_rows, 128), F32)
    maps = ((4, padded, width), BF16)
    lane_maps = ((width // 128, 2 * chans, 128), F32)
    maps_in = ((2, chans, 2, width), BF16)
    one_up, one_down = ((1, width, hidden_size), BF16), ((1, hidden_size, width), BF16)

    smem, args, outs = (), (), []
    if packed:
        smem = (obs_counts,)
        args = tuple(x.reshape(lanes, 128) for x in (obs_cells, obs_chans, obs_values))
        outs = [((lanes * 4, 128), F32)]
    hidden, first, last, *pay, xp, w = call(
        functools.partial(embed_kernel, lon_size if packed else None),
        [((tokens, width), BF16), halo, halo] + outs,
        [
            rows_f32, ((tokens, 4 * padded), BF16), maps, by_cell,
            ((chans, lon_rows, lat), BF16), maps_in, lane_maps,
        ],
        5, cells // half + 1, (2 * tokens * 12 * padded * width, 4 * state.size),
        smem, args, (state, w), (by_cell, maps),
    )
    low = lax.ppermute(last, "lon", forward)
    high = lax.ppermute(first, "lon", backward)
    if packed:
        sent = pay[0].reshape(lon_size, 4 * per_peer // 128, 128)
    else:
        tile_lon, tile_lat = obs_cells // lat, obs_cells % lat
        place = (tile_lon % 2 * 2 + tile_lat % 2) * patch_rows + tile_lon // 2
        place = place * half + tile_lat // 2
        live = (jnp.arange(slots, dtype=jnp.int32) < obs_counts[0]).astype(F32)
        sent = jnp.stack(
            [
                part.astype(F32).reshape(lon_size, per_peer)
                for part in (place, obs_chans, obs_values, live)
            ],
            axis=1,
        )
    pay = lax.all_to_all(sent, "lon", split_axis=0, concat_axis=0, tiled=True)
    if not packed:
        group = BLOCK // per_peer
        pay = pay.reshape(lon_size // group, group, 4, per_peer)
        pay = jnp.transpose(pay, (0, 2, 1, 3)).reshape(lon_size // group, 8, 128)
    table, unit0, scale0, slope0, unit1, scale1, slope1, u = call(
        forward_kernel,
        [],
        [
            ((patch_rows + 2 * HALO, half, width), BF16),
            ((patch_rows + 2, half, width), BF16),
            fat,
            ((wide, width), BF16),
            ((tokens, width), BF16),
            maps, by_cell, maps_in,
            (mlp_up.shape, BF16), (mlp_down.shape, BF16),
            by_cell, fat_unit, fat_scale, fat_slope, thin_unit, thin_scale, thin_slope,
            lane_maps,
        ],
        6, 11, (3 * 10**9, 10**7),
        (), (hidden, low, high, taps, conv_bias, norm_gain), (xp, u, mlp_up, mlp_down),
        (by_cell, fat_unit, fat_scale, fat_slope, thin_unit, thin_scale, thin_slope, maps),
    )
    innov, grad, first, last, grad_t, denoised = call(
        radiance_kernel,
        [((lanes, 128), F32), ((tokens, width), BF16), halo, halo],
        [
            ((emu // 128, padded, 128), BF16),
            ((padded // 128, emu, 128), BF16),
            ((emu // 128, head_pad, 128), BF16),
            ((emu, 128), F32),
            ((lanes, half, 128), BF16),
            ((lanes, padded, 128), BF16),
            ((padded // 128, cells, 128), BF16),
            maps, rows_f32, ((chans, lon_rows, lat), BF16),
            ((padded, BLOCK), BF16), ((emu, BLOCK), GELU), ((emu, BLOCK), F32),
            ((8, BLOCK), F32), ((emu, BLOCK), BF16),
            by_cell, one_up, one_down, thin_unit, thin_scale, thin_slope, by_cell,
        ],
        7, 2, (14 * 10**9, 10**7),
        (),
        (pay, emu_encode, chan_table, chan_head, head_bias.reshape(1, nchan), norm_gain),
        (table, u, mlp_up, mlp_down, unit1, scale1, slope1),
        (by_cell, ((chans, lon_rows, lat), BF16)),
    )
    back = lax.ppermute(last, "lon", forward)
    ahead = lax.ppermute(first, "lon", backward)
    if packed:
        innov = innov.reshape(lon_size, per_peer // 128, 128)
    else:
        innov = innov.reshape(lon_size, per_peer)
    innovations = lax.all_to_all(innov, "lon", split_axis=0, concat_axis=0, tiled=True)
    (out,) = call(
        last_kernel,
        [],
        [
            ((patch_rows + 2 * HALO, half, width), BF16),
            fat,
            ((patch_rows + 2, half, width), BF16),
            ((tokens, width), BF16),
            by_cell, rows_f32, maps,
            fat_unit, fat_scale, fat_slope, by_cell, one_up, one_down,
        ],
        4 + 3 * (patch_rows + 2) // 2, 2 * (lat // 128), (4 * 10**9, 10**7),
        (), (grad, back, ahead, taps, norm_gain),
        (unit0, scale0, slope0, grad_t, w, mlp_up, mlp_down),
        (((chans * lon_rows, lat), F32),),
    )
    state_gradient = jnp.transpose(out.reshape(chans, lon_rows, lat), (1, 0, 2))
    return (jnp.transpose(denoised, (1, 0, 2)), state_gradient, innovations.reshape(slots))


def solution(mesh):
    split = P(("groups", "lon"))
    placed = (split,) + (P(),) * 11 + (split,) * 4
    return jax.shard_map(
        shards, mesh=mesh, in_specs=placed, out_specs=(split,) * 3, check_vma=False
    )
```
